128 devices in a mesh: row: 8 (over x, core), col: 16 (over y, z).
Axes of the slice: x: 4, y: 4, z: 4, core: 2. Of those that a mesh axis runs over, the one named last changes fastest.
Arguments:
- a_matrix: float32 [32768, 24576], P('row', 'col'), may hold values from 0 to 1
- h_factor: float32 [256, 24576], P(None, 'col'), may hold values from 0 to 1
- w_factor: float32 [32768, 256], P('row'), may hold values from 0 to 0.0078125
- accept: int32 [32768, 2], P('row'), may hold values from 0 to 1
- shrink: int32 [32768, 2], P('row'), may hold values from 0 to 3
Outputs:
- w_new: float32 [32768, 256], P('row')
- grad_h: float32 [256, 24576], P('row', 'col')
- armijo: float32 [2, 2], replicated
The draws below stay inside these ranges and needn't reach their ends.
All inputs are finite; a program needn't handle non-finite values.
Results may differ from the reference program's by a relative error of at most 0.00012.
Values sent between devices are 32-bit elements; how exact they have to be, the bound alone decides.
A program may use at most 192 MiB of HBM per device.

```python
import jax
import jax.numpy as jnp
from jax import lax

K = 256
TRIALS = 2
M = 32768
N = 24576


def plant(array, stream_key, low, high):
    shape = array.shape
    index_at = [jax.random.randint(jax.random.fold_in(stream_key, axis), (), 0, shape[axis]) for axis in range(len(shape))]
    array = array.at[tuple(index_at)].set(low)
    longest = shape.index(max(shape))
    index_at[longest] = (index_at[longest] + 1) % shape[longest]
    return array.at[tuple(index_at)].set(high)


def block_levels(key, dims, split, low, top_value):
    factor_of, own = 1.0, jax.random.fold_in(key, 6)
    for axis_at, parts in split:
        heights = jnp.exp(jax.random.uniform(jax.random.fold_in(own, axis_at), (parts,), jnp.float32, low / len(split), top_value / len(split)))
        factor_of = factor_of * jnp.repeat(heights, dims[axis_at] // parts).reshape([-1 if axis == axis_at else 1 for axis in range(len(dims))])
    return factor_of


def setup_inputs(seed: int = 0) -> dict:
    key_of = jax.random.split(jax.random.key(seed), 6)
    a_matrix = jnp.clip(1.0 * jax.random.uniform(key_of[0], (M, N), jnp.float32) ** block_levels(key_of[0], (M, N), ((0, 8), (1, 16)), -0.2, 0.2), 0.0, 1.0)
    h_factor = jnp.clip(1.0 * jax.random.uniform(key_of[1], (K, N), jnp.float32) ** block_levels(key_of[1], (K, N), ((1, 16),), -0.2, 0.2), 0.0, 1.0)
    w_factor = jnp.clip(0.0078125 * jax.random.uniform(key_of[2], (M, K), jnp.float32) ** block_levels(key_of[2], (M, K), ((0, 8),), -0.2, 0.2), 0.0, 0.0078125)
    accept = plant(jax.random.randint(key_of[3], (M, TRIALS), 0, 2), jax.random.fold_in(key_of[3], 1), 0, 1).astype(jnp.int32)
    shrink = plant(jax.random.randint(key_of[4], (M, TRIALS), 0, 4), jax.random.fold_in(key_of[4], 1), 0, 3).astype(jnp.int32)
    return dict(a_matrix=a_matrix, h_factor=h_factor, w_factor=w_factor, accept=accept, shrink=shrink)


def reference(a_matrix, h_factor, w_factor, accept, shrink):
    highest = lax.Precision.HIGHEST
    hh = jnp.dot(h_factor, h_factor.T, precision=highest, preferred_element_type=jnp.float32)
    ah = jnp.dot(a_matrix, h_factor.T, precision=highest, preferred_element_type=jnp.float32)
    step_size = K / jnp.trace(hh)
    current = w_factor
    flags = accept.astype(jnp.float32)
    powers = shrink.astype(jnp.float32)
    results = []
    for trial in range(TRIALS):
        gradient = jnp.dot(current, hh, precision=highest, preferred_element_type=jnp.float32) - ah
        factor = jnp.power(jnp.float32(0.5), powers[:, trial:trial + 1]) * step_size
        change = jnp.maximum(current - factor * gradient, 0.0) - current
        first = jnp.sum(gradient * change)
        second = jnp.sum(change * jnp.dot(change, hh, precision=highest, preferred_element_type=jnp.float32))
        results.append(jnp.stack([first, second]))
        current = current + flags[:, trial:trial + 1] * change
    residue = jnp.dot(current, h_factor, precision=highest, preferred_element_type=jnp.float32) - a_matrix
    grad_h = jnp.dot(current.T, residue, precision=highest, preferred_element_type=jnp.float32)
    return current, grad_h, jnp.stack(results)
```

```python
import functools

import jax
import jax.numpy as jnp
from jax import lax
from jax.experimental import pallas as pl
from jax.experimental.pallas import tpu as pltpu
from jax.sharding import PartitionSpec as P

F32, BF16 = jnp.float32, jnp.bfloat16
MESH = pl.DeviceIdType.MESH
RANK, ROWS, COLS = 256, 4096, 1536
PIECE, GROUP, FLOW = 128, 512, 2048
TILES = 3
WIDTH = COLS // TILES
RELAY = (((2, 1), (3, 0)))


def halves(x):
    hi = x.astype(BF16)
    return hi, (x - hi.astype(F32)).astype(BF16)


def mm(a, b):
    return lax.dot_general(a, b, (((1,), (0,)), ((), ())), preferred_element_type=F32)


def exact(a, b):
    return jnp.dot(a, b, precision=lax.Precision.HIGHEST, preferred_element_type=F32)


def sem_keys():
    keys = []
    for f in range(2):
        for d in range(2):
            keys += [("ra", f, d, r) for r in RELAY[d]]
            keys += [("rb", f, d, r) for r in range(4)]
            keys += [("rc", f, d), ("rd", f, d, 0), ("rd", f, d, 1)]
            keys += [("g1", f, d), ("g1h", f, d)]
            keys += [("g2", f, d, r) for r in range(4)]
            keys += [("g2h", f, d, r) for r in range(4)]
    for name, count in (("s1", 4), ("s2", 4), ("s3", 4), ("s4", 8), ("a1", 8), ("a2", 4), ("a3", 4)):
        keys += [(name, d) for d in range(1, count)]
    for t in range(TILES):
        keys += [("core", t, k) for k in range(4)]
        for d in range(2):
            keys += [("ga", t, d), ("gb", t, d, 0), ("gb", t, d, 1)]
    return {key: at for at, key in enumerate(keys)}


KEYS = sem_keys()


def kernel(
    a_hbm, h_hbm, w_hbm, accept_hbm, shrink_hbm,
    w_out, g_out, stat_out,
    a_buf, a_hi, a_lo, h_f32, ht_hi, ht_lo, h_hi, h_lo,
    ah, ra, rb, rc, rd,
    gram, s1, s2, hh_buf,
    w_own, flags_raw, powers_raw, flags, factors, base,
    wg, acc, wtw, core_in, ga, gb, a1, a2, a3,
    send_sem, recv_sem, a_sem, in_sem, w_sem,
):
    rho, col = lax.axis_index("row"), lax.axis_index("col")
    y, z = lax.div(col, 4), lax.rem(col, 4)
    x, core = lax.div(rho, 2), lax.rem(rho, 2)
    along, across = (y, z), (z, y)

    def at_y(d):
        return (rho, lax.rem(y + d, 4) * 4 + z)

    def at_z(d):
        return (rho, y * 4 + lax.rem(z + d, 4))

    def at_row(d):
        return (lax.rem(rho + d, 8), col)

    def at_x(d):
        return (lax.rem(x + d, 4) * 2 + core, col)

    partner = (x * 2 + 1 - core, col)
    step_p, step_q = (at_y, at_z), (at_z, at_y)
    way = (1, 3)

    def row(f, dp, dq):
        return pl.multiple_of(
            f * FLOW + GROUP * lax.rem(along[f] + dp, 4) + PIECE * lax.rem(across[f] + dq, 4), PIECE
        )

    def piece(ref, f, dp, dq, start=0, size=PIECE):
        return ref.at[pl.ds(pl.multiple_of(row(f, dp, dq) + start, 64), size), :]

    sent = []

    def make(key, src, dst, to):
        return pltpu.make_async_remote_copy(
            src_ref=src, dst_ref=dst, send_sem=send_sem.at[KEYS[key]], recv_sem=recv_sem.at[KEYS[key]],
            device_id=to, device_id_type=MESH,
        )

    def send(key, src, dst, to):
        make(key, src(), dst(), to()).start()
        sent.append((key, src, dst, to))

    def arrived(key, dst, to):
        make(key, dst, dst, to).wait_recv()

    def chunk_row(j):
        f, t = lax.rem(j, 2), lax.div(j, 2)
        dp = 2 - t + 3 * lax.div(t, 2) - 2 * lax.div(t, 3)
        return pl.multiple_of(f * FLOW + GROUP * lax.rem(y + f * (z - y) + dp, 4), GROUP)

    def a_copy(j):
        slot = lax.rem(j, 2)
        return pltpu.make_async_copy(a_hbm.at[pl.ds(chunk_row(j), GROUP), :], a_buf.at[slot], a_sem.at[slot])

    h_copy = pltpu.make_async_copy(h_hbm, h_f32, in_sem.at[0])
    h_copy.start()
    a_copy(jnp.int32(0)).start()
    small = [
        pltpu.make_async_copy(accept_hbm, flags_raw, in_sem.at[1]),
        pltpu.make_async_copy(shrink_hbm, powers_raw, in_sem.at[2]),
        pltpu.make_async_copy(piece(w_hbm, 0, 0, 0), w_own.at[pl.ds(0, PIECE), :], in_sem.at[3]),
        pltpu.make_async_copy(piece(w_hbm, 1, 0, 0), w_own.at[pl.ds(PIECE, PIECE), :], in_sem.at[4]),
    ]
    for copy in small:
        copy.start()
    a_copy(jnp.int32(1)).start()

    barrier = pltpu.get_barrier_semaphore()
    peers = [at_row(d) for d in range(1, 8)] + [at_y(d) for d in range(1, 4)] + [at_z(d) for d in range(1, 4)]
    for peer in peers:
        pl.semaphore_signal(barrier, inc=1, device_id=peer, device_id_type=MESH)

    h_copy.wait()
    for n in range(COLS // 256):
        block = h_f32[:, n * 256 : (n + 1) * 256]
        hi, lo = halves(block)
        h_hi[:, n * 256 : (n + 1) * 256] = hi
        h_lo[:, n * 256 : (n + 1) * 256] = lo
        hi, lo = halves(block.T)
        ht_hi[n * 256 : (n + 1) * 256, :] = hi
        ht_lo[n * 256 : (n + 1) * 256, :] = lo
    part_hi, part_lo = halves(h_f32[pl.ds(pl.multiple_of(rho * 32, 32), 32), :])
    gram[...] = (
        mm(part_hi, ht_hi[...]) + mm(part_hi, ht_lo[...]) + mm(part_lo, ht_hi[...]) + mm(part_lo, ht_lo[...])
    )
    s1[y] = gram[pl.ds(pl.multiple_of(8 * y, 8), 8), :]
    pl.semaphore_wait(barrier, len(peers))

    def gram_rows(d):
        return gram.at[pl.ds(pl.multiple_of(8 * lax.rem(y + d, 4), 8), 8), :]

    for d in range(1, 4):
        send(("s1", d), lambda d=d: gram_rows(d), lambda: s1.at[y], lambda d=d: at_y(d))

    def gram_z():
        for d in range(1, 4):
            arrived(("s1", d), s1.at[lax.rem(y + 4 - d, 4)], at_y(d))
        s2[z] = s1[0] + s1[1] + s1[2] + s1[3]
        for d in range(1, 4):
            send(("s2", d), lambda: s2.at[z], lambda: s2.at[z], lambda d=d: at_z(d))

    def hh_rows(r, k):
        return hh_buf.at[r, pl.ds(pl.multiple_of(8 * k, 8), 8), :]

    def gram_y():
        for d in range(1, 4):
            arrived(("s2", d), s2.at[lax.rem(z + 4 - d, 4)], at_z(d))
        hh_buf[rho, pl.ds(pl.multiple_of(8 * y, 8), 8), :] = s2[0] + s2[1] + s2[2] + s2[3]
        for d in range(1, 4):
            send(("s3", d), lambda: hh_rows(rho, y), lambda: hh_rows(rho, y), lambda d=d: at_y(d))

    def gram_row():
        for d in range(1, 4):
            arrived(("s3", d), hh_rows(rho, lax.rem(y + 4 - d, 4)), at_y(d))
        for d in range(1, 8):
            send(("s4", d), lambda: hh_buf.at[rho], lambda: hh_buf.at[rho], lambda d=d: at_row(d))

    def opposite(f):
        for d in range(2):
            for i, r in enumerate(RELAY[d]):
                send(("ra", f, d, r), lambda r=r: piece(ah, f, 2, r), lambda d=d, i=i: ra.at[f, d, i],
                     lambda d=d: step_p[f](way[d]))

    def near(f, d, r):
        send(("rb", f, d, r), lambda: piece(ah, f, way[d], r), lambda: rb.at[f, d, r], lambda: step_p[f](way[d]))

    def alone(f, d):
        for r in RELAY[1 - d]:
            near(f, d, r)

    def relayed(f):
        for i in range(2):
            for d in range(2):
                r = RELAY[d][i]
                arrived(("ra", f, d, r), ra.at[f, d, i], step_p[f](way[d]))
                at = pl.ds(row(f, way[d], r), PIECE)
                ah[at, :] += ra[f, d, i]
                near(f, d, r)

    hooks = {
        0: [gram_z, lambda: opposite(0)],
        1: [lambda: opposite(1)],
        2: [gram_y, lambda: alone(0, 0)],
        3: [lambda: alone(1, 0)],
        4: [lambda: alone(0, 1)],
        5: [lambda: alone(1, 1), lambda: relayed(0)],
        6: [lambda: relayed(1), gram_row],
    }

    @pl.loop(0, 8)
    def _(j):
        slot = lax.rem(j, 2)
        at = pl.ds(chunk_row(j), GROUP)
        a_copy(j).wait()
        hi, lo = halves(a_buf[slot])
        a_hi[at, :] = hi
        a_lo[at, :] = lo

        @pl.when(j < 6)
        def _():
            a_copy(j + 2).start()

        ah[at, :] = mm(a_hi[at, :], ht_hi[...]) + mm(a_hi[at, :], ht_lo[...]) + mm(a_lo[at, :], ht_hi[...])
        for when, steps in hooks.items():

            @pl.when(j == when)
            def _(steps=steps):
                for step in steps:
                    step()

    for copy in small:
        copy.wait()
    acc[...] = jnp.zeros_like(acc)
    wtw[...] = jnp.zeros_like(wtw)

    def down(line):
        return jnp.broadcast_to(line, (PIECE, PIECE)).T

    for f in range(2):
        lanes = pl.ds(row(f, 0, 0), PIECE)
        for t in range(2):
            at = slice(f * PIECE, (f + 1) * PIECE)
            flags[t, at, :] = down(flags_raw[t : t + 1, lanes].astype(F32))
            power = powers_raw[t : t + 1, lanes]
            scale = jnp.where(power == 0, 1.0, jnp.where(power == 1, 0.5, jnp.where(power == 2, 0.25, 0.125)))
            factors[t, at, :] = down(scale.astype(F32))

    for d in range(1, 8):
        arrived(("s4", d), hh_buf.at[lax.rem(rho + 8 - d, 8)], at_row(d))
    hh = hh_buf[...].reshape(RANK, RANK)
    base[...] = exact(w_own[...], hh)

    def own_sum(f, r):
        for d in range(2):
            arrived(("rb", f, d, r), rb.at[f, d, r], step_p[f](way[d]))
        at = pl.ds(row(f, 0, r), PIECE)
        ah[at, :] += rb[f, 0, r] + rb[f, 1, r]

    def half(f, r, start):
        return lambda: piece(ah, f, 0, r, start, 64)

    for f in range(2):
        own_sum(f, 2)
        for d in range(2):
            send(("rc", f, d), half(f, 2, 64 * d), lambda f=f, d=d: rc.at[f, d], lambda f=f, d=d: step_q[f](way[d]))

    def last(f, d, part):
        start = 64 * d if part == 0 else 64 * (1 - d)
        send(("rd", f, d, part), half(f, way[d], start), lambda: rd.at[f, d, pl.ds(start, 64), :],
             lambda: step_q[f](way[d]))

    for d, r in ((1, 3), (0, 1)):
        for f in range(2):
            own_sum(f, r)
            last(f, d, 1)
    for f in range(2):
        own_sum(f, 0)
    for f in range(2):
        for d in range(2):
            arrived(("rc", f, d), rc.at[f, d], step_q[f](way[d]))
            at = pl.ds(pl.multiple_of(row(f, 0, way[d]) + 64 * d, 64), 64)
            ah[at, :] += rc[f, d]
            last(f, d, 0)
    for f in range(2):
        for d in range(2):
            for part in range(2):
                start = 64 * d if part == 0 else 64 * (1 - d)
                arrived(("rd", f, d, part), rd.at[f, d, pl.ds(start, 64), :], step_q[f](way[d]))
    own = [pl.ds(row(f, 0, 0), PIECE) for f in range(2)]
    total = jnp.concatenate([ah[own[f], :] + rd[f, 0] + rd[f, 1] for f in range(2)], axis=0)

    both = (RANK, RANK)
    eye = lax.broadcasted_iota(jnp.int32, both, 0) == lax.broadcasted_iota(jnp.int32, both, 1)
    step_size = float(RANK) / jnp.sum(jnp.where(eye, hh, 0.0), keepdims=True)

    def twice(v):
        return jnp.concatenate([v, v], axis=1)

    current = w_own[...]
    gradient = base[...] - total
    sums = []
    for t in range(2):
        change = jnp.maximum(current - twice(factors[t]) * step_size * gradient, 0.0) - current
        sums.append(jnp.sum(gradient * change, keepdims=True))
        current = current + twice(flags[t]) * change
        if t == 0:
            turned = exact(change, hh)
            sums.append(jnp.sum(change * turned, keepdims=True))
            gradient = gradient + twice(flags[t]) * turned
    for f in range(2):
        wg[own[f], :] = current[f * PIECE : (f + 1) * PIECE]

    for f in range(2):
        for d in range(2):
            send(("g1", f, d), lambda f=f: piece(wg, f, 0, 0), lambda f=f: piece(wg, f, 0, 0),
                 lambda f=f, d=d: step_q[f](way[d]))

    def spread(f, r):
        for d in range(2):
            send(("g2", f, d, r), lambda: piece(wg, f, 0, r), lambda: piece(wg, f, 0, r),
                 lambda d=d: step_p[f](way[d]))

    for f in range(2):
        spread(f, 0)
    sums.append(jnp.sum(change * exact(change, hh), keepdims=True))
    line = lax.broadcasted_iota(jnp.int32, (8, 128), 0)
    stats = jnp.zeros((8, 128), F32)
    for at, value in enumerate(sums):
        stats = jnp.where(line == at, value, stats)
    a1[rho] = stats
    for d in range(1, 8):
        send(("a1", d), lambda: a1.at[rho], lambda: a1.at[rho], lambda d=d: at_row(d))

    def stats_y():
        for d in range(1, 8):
            arrived(("a1", d), a1.at[lax.rem(rho + 8 - d, 8)], at_row(d))
        a2[y] = sum(a1[k] for k in range(1, 8)) + a1[0]
        for d in range(1, 4):
            send(("a2", d), lambda: a2.at[y], lambda: a2.at[y], lambda d=d: at_y(d))

    def stats_z():
        for d in range(1, 4):
            arrived(("a2", d), a2.at[lax.rem(y + 4 - d, 4)], at_y(d))
        a3[z] = a2[0] + a2[1] + a2[2] + a2[3]
        for d in range(1, 4):
            send(("a3", d), lambda: a3.at[z], lambda: a3.at[z], lambda d=d: at_z(d))

    def beside(f):
        for d in range(2):
            r = 4 - way[d]
            arrived(("g1", f, d), piece(wg, f, 0, r), step_q[f](way[d]))
            send(("g1h", f, d), lambda r=r, d=d: piece(wg, f, 0, r, 64 * d, 64),
                 lambda r=r, d=d: piece(wg, f, 0, r, 64 * d, 64), lambda d=d: step_q[f](way[d]))
        for r in (1, 3):
            spread(f, r)

    def across_ring(f):
        for d in range(2):
            arrived(("g1h", f, d), piece(wg, f, 0, 2, 64 * d, 64), step_q[f](way[d]))
        spread(f, 2)

    def onward(f, r):
        for d in range(2):
            dp = 4 - way[d]
            arrived(("g2", f, d, r), piece(wg, f, dp, r), step_p[f](way[d]))
            send(("g2h", f, d, r), lambda dp=dp, d=d: piece(wg, f, dp, r, 64 * d, 64),
                 lambda dp=dp, d=d: piece(wg, f, dp, r, 64 * d, 64), lambda d=d: step_p[f](way[d]))

    def far(f, r):
        for d in range(2):
            arrived(("g2h", f, d, r), piece(wg, f, 2, r, 64 * d, 64), step_p[f](way[d]))

    def w_copy(f, dp):
        at = pl.ds(pl.multiple_of(f * FLOW + GROUP * lax.rem(along[f] + dp, 4), GROUP), GROUP)
        return pltpu.make_async_copy(wg.at[at, :], w_out.at[at, :], w_sem.at[f * 4 + dp])

    def store(dp):
        for f in range(2):
            w_copy(f, dp).start()

    def pair(step, *given):
        return lambda: [step(f, *given) for f in range(2)]

    before = {
        1: [pair(beside)],
        2: [stats_y],
        3: [pair(across_ring), lambda: store(0)],
        4: [pair(onward, 0)],
        6: [pair(onward, 1)],
        8: [pair(onward, 3), stats_z],
        10: [pair(onward, 2), lambda: store(1), lambda: store(3)],
        12: [pair(far, 0)],
        13: [pair(far, 1)],
        14: [pair(far, 3)],
        15: [pair(far, 2), lambda: store(2)],
    }

    @pl.loop(0, 16)
    def _(u):
        for when, steps in before.items():

            @pl.when(u == when)
            def _(steps=steps):
                for step in steps:
                    step()

        e = lax.div(lax.div(u, 4) + 1, 2)
        e0, e1, e2 = 1 - lax.div(e + 1, 2), lax.rem(e, 2), lax.div(e, 2)
        dp = e1 * (1 + 2 * lax.rem(u, 2)) + e2 * 2
        k = e0 * u + e1 * lax.div(u - 4, 2) + e2 * (u - 12)
        r = k + lax.div(k, 2) - 2 * lax.div(k, 3)
        at = [pl.ds(row(f, dp, r), PIECE) for f in range(2)]

        w = jnp.concatenate([wg[at[0], :], wg[at[1], :]], axis=0)
        w_hi, w_lo = halves(w)
        t_hi, t_lo = halves(w.T)
        left = jnp.concatenate([t_hi, t_lo], axis=0)
        for t in range(TILES):
            cols = slice(t * WIDTH, (t + 1) * WIDTH)
            m_hi = jnp.concatenate([a_hi[at[0], cols], a_hi[at[1], cols]], axis=0)
            m_lo = jnp.concatenate([a_lo[at[0], cols], a_lo[at[1], cols]], axis=0)
            two = mm(left, m_hi)
            acc[t] += two[:RANK] + two[RANK:] + mm(t_hi, m_lo)
        two = mm(left, w_hi)
        wtw[...] += two[:RANK] + two[RANK:] + mm(t_hi, w_lo)

    def block(t, k, mine, start=0, size=32):
        at = 64 * lax.rem(x + k, 4) + 32 * (core if mine else 1 - core) + start
        return (t, pl.ds(pl.multiple_of(at, 16), size), slice(None))

    q_hi, q_lo = halves(wtw[...])

    def finish(t):
        cols = slice(t * WIDTH, (t + 1) * WIDTH)
        acc[t] = mm(q_hi, h_hi[:, cols]) + mm(q_hi, h_lo[:, cols]) + mm(q_lo, h_hi[:, cols]) - acc[t]
        for k in (2, 1, 3, 0):
            send(("core", t, k), lambda k=k: acc.at[block(t, k, False)], lambda k=k: core_in.at[t, k], lambda: partner)

    def joined(t, k):
        arrived(("core", t, k), core_in.at[t, k], partner)
        acc[block(t, k, True)] += core_in[t, k]

    def first(t):
        joined(t, 2)
        for d in range(2):
            send(("ga", t, d), lambda d=d: acc.at[block(t, 2, True, 16 * d, 16)], lambda d=d: ga.at[t, d],
                 lambda d=d: at_x(way[d]))
        for d in range(2):
            joined(t, way[d])
            onto(t, d, 1)
        joined(t, 0)

    def onto(t, d, part):
        start = 16 * d if part == 0 else 16 * (1 - d)
        send(("gb", t, d, part), lambda: acc.at[block(t, way[d], True, start, 16)],
             lambda: gb.at[t, d, pl.ds(start, 16), :], lambda: at_x(way[d]))

    def second(t):
        for d in range(2):
            arrived(("ga", t, d), ga.at[t, d], at_x(way[d]))
            acc[block(t, way[d], True, 16 * d, 16)] += ga[t, d]
            onto(t, d, 0)

    def third(t):
        for d in range(2):
            for part in range(2):
                start = 16 * d if part == 0 else 16 * (1 - d)
                arrived(("gb", t, d, part), gb.at[t, d, pl.ds(start, 16), :], at_x(way[d]))
        g_out[:, t * WIDTH : (t + 1) * WIDTH] = acc[block(t, 0, True)] + gb[t, 0] + gb[t, 1]

    for t in range(TILES):
        finish(t)
    for t in range(TILES):
        first(t)
    for t in range(TILES):
        second(t)
    for d in range(1, 4):
        arrived(("a3", d), a3.at[lax.rem(z + 4 - d, 4)], at_z(d))
    stat_out[...] = a3[0] + a3[1] + a3[2] + a3[3]
    for t in range(TILES):
        third(t)
    for f in range(2):
        for dp in range(4):
            w_copy(f, dp).wait()
    for key, src, dst, to in sent:
        make(key, src(), dst(), to()).wait_send()


def per_device(a_matrix, h_factor, w_factor, accept, shrink):
    vmem = pltpu.VMEM
    anywhere = pl.BlockSpec(memory_space=pl.ANY)
    inside = pl.BlockSpec(memory_space=vmem)
    w_new, grad_h, stats = pl.pallas_call(
        kernel,
        out_shape=(
            jax.ShapeDtypeStruct((ROWS, RANK), F32),
            jax.ShapeDtypeStruct((RANK // 8, COLS), F32),
            jax.ShapeDtypeStruct((8, 128), F32),
        ),
        in_specs=[anywhere] * 5,
        out_specs=(anywhere, inside, inside),
        scratch_shapes=[
            vmem((2, GROUP, COLS), F32),
            vmem((ROWS, COLS), BF16),
            vmem((ROWS, COLS), BF16),
            vmem((RANK, COLS), F32),
            vmem((COLS, RANK), BF16),
            vmem((COLS, RANK), BF16),
            vmem((RANK, COLS), BF16),
            vmem((RANK, COLS), BF16),
            vmem((ROWS, RANK), F32),
            vmem((2, 2, 2, PIECE, RANK), F32),
            vmem((2, 2, 4, PIECE, RANK), F32),
            vmem((2, 2, 64, RANK), F32),
            vmem((2, 2, PIECE, RANK), F32),
            vmem((32, RANK), F32),
            vmem((4, 8, RANK), F32),
            vmem((4, 8, RANK), F32),
            vmem((8, 32, RANK), F32),
            vmem((RANK, RANK), F32),
            vmem((2, ROWS), jnp.int32),
            vmem((2, ROWS), jnp.int32),
            vmem((2, RANK, PIECE), F32),
            vmem((2, RANK, PIECE), F32),
            vmem((RANK, RANK), F32),
            vmem((ROWS, RANK), F32),
            vmem((TILES, RANK, WIDTH), F32),
            vmem((RANK, RANK), F32),
            vmem((TILES, 4, 32, WIDTH), F32),
            vmem((TILES, 2, 16, WIDTH), F32),
            vmem((TILES, 2, 32, WIDTH), F32),
            vmem((8, 8, 128), F32),
            vmem((4, 8, 128), F32),
            vmem((4, 8, 128), F32),
            pltpu.SemaphoreType.DMA((len(KEYS),)),
            pltpu.SemaphoreType.DMA((len(KEYS),)),
            pltpu.SemaphoreType.DMA((2,)),
            pltpu.SemaphoreType.DMA((5,)),
            pltpu.SemaphoreType.DMA((8,)),
        ],
        compiler_params=pltpu.CompilerParams(
            collective_id=0, has_side_effects=True, vmem_limit_bytes=67043328
        ),
    )(a_matrix, h_factor, w_factor, accept.T, shrink.T)
    return w_new, grad_h, stats[:4, 0].reshape(2, 2)


def solution(mesh):
    in_specs = (P("row", "col"), P(None, "col"), P("row", None), P("row", None), P("row", None))
    out_specs = (P("row", None), P("row", "col"), P())
    return jax.shard_map(per_device, mesh=mesh, in_specs=in_specs, out_specs=out_specs, check_vma=False)
```

```python
import functools

import jax
import jax.numpy as jnp
from jax import lax
from jax.experimental import pallas as pl
from jax.experimental.pallas import tpu as pltpu
from jax.sharding import PartitionSpec as P

F32, BF16 = jnp.float32, jnp.bfloat16
MESH = pl.DeviceIdType.MESH
RANK, ROWS, COLS = 256, 4096, 1536
PIECE, GROUP, FLOW = 128, 512, 2048
TILES = 3
WIDTH = COLS // TILES
RELAY = (((2, 1), (3, 0)))


def halves(x):
    hi = x.astype(BF16)
    return hi, (x - hi.astype(F32)).astype(BF16)


def mm(a, b):
    return lax.dot_general(a, b, (((1,), (0,)), ((), ())), preferred_element_type=F32)


def mmt(a, b):
    return lax.dot_general(a, b, (((1,), (1,)), ((), ())), preferred_element_type=F32)


def exact(a, b):
    return jnp.dot(a, b, precision=lax.Precision.HIGHEST, preferred_element_type=F32)


def sem_keys():
    keys = []
    for f in range(2):
        for d in range(2):
            keys += [("ra", f, d, r) for r in RELAY[d]]
            keys += [("rb", f, d, r) for r in range(4)]
            keys += [("rc", f, d), ("rd", f, d, 0), ("rd", f, d, 1)]
            keys += [("g1", f, d), ("g1h", f, d)]
            keys += [("g2", f, d, r) for r in range(4)]
            keys += [("g2h", f, d, r) for r in range(4)]
    for name, count in (("s1", 4), ("s2", 4), ("s4", 8), ("t1", 8), ("t2", 4), ("t3", 4), ("t4", 4), ("a1", 8), ("a2", 4), ("a3", 4)):
        keys += [(name, d) for d in range(1, count)]
    for t in range(TILES):
        keys += [("core", t, k) for k in range(4)]
        for d in range(2):
            keys += [("ga", t, d), ("gb", t, d, 0), ("gb", t, d, 1)]
    return {key: at for at, key in enumerate(keys)}


KEYS = sem_keys()


def kernel(
    a_hbm, h_hbm, w_hbm, accept_hbm, shrink_hbm,
    wg, g_out, stat_out,
    a_buf, a_hi, a_lo, h_f32, h_hi, h_lo,
    ah, ra, rb, rc, rd,
    s1, s2, t1, t_sum, t2, t3, t_all, hh_buf,
    w_own, flags_raw, powers_raw, flags, factors, base,
    acc, wtw, core_in, ga, gb, a1, a2, a3,
    send_sem, recv_sem, a_sem, in_sem,
):
    rho, col = lax.axis_index("row"), lax.axis_index("col")
    y, z = lax.div(col, 4), lax.rem(col, 4)
    x, core = lax.div(rho, 2), lax.rem(rho, 2)
    along, across = (y, z), (z, y)

    def at_y(d):
        return (rho, lax.rem(y + d, 4) * 4 + z)

    def at_z(d):
        return (rho, y * 4 + lax.rem(z + d, 4))

    def at_row(d):
        return (lax.rem(rho + d, 8), col)

    def at_x(d):
        return (lax.rem(x + d, 4) * 2 + core, col)

    partner = (x * 2 + 1 - core, col)
    step_p, step_q = (at_y, at_z), (at_z, at_y)
    way = (1, 3)

    def row(f, dp, dq):
        return pl.multiple_of(
            f * FLOW + GROUP * lax.rem(along[f] + dp, 4) + PIECE * lax.rem(across[f] + dq, 4), PIECE
        )

    def piece(ref, f, dp, dq, start=0, size=PIECE):
        return ref.at[pl.ds(pl.multiple_of(row(f, dp, dq) + start, 64), size), :]

    sent = []

    def make(key, src, dst, to):
        return pltpu.make_async_remote_copy(
            src_ref=src, dst_ref=dst, send_sem=send_sem.at[KEYS[key]], recv_sem=recv_sem.at[KEYS[key]],
            device_id=to, device_id_type=MESH,
        )

    def send(key, src, dst, to):
        make(key, src(), dst(), to()).start()
        sent.append((key, src, dst, to))

    def arrived(key, dst, to):
        make(key, dst, dst, to).wait_recv()

    def chunk_row(j):
        f, t = lax.rem(j, 2), lax.div(j, 2)
        dp = 2 - t + 3 * lax.div(t, 2) - 2 * lax.div(t, 3)
        return pl.multiple_of(f * FLOW + GROUP * lax.rem(y + f * (z - y) + dp, 4), GROUP)

    def a_copy(j):
        slot = lax.rem(j, 2)
        return pltpu.make_async_copy(a_hbm.at[pl.ds(chunk_row(j), GROUP), :], a_buf.at[slot], a_sem.at[slot])

    h_copy = pltpu.make_async_copy(h_hbm, h_f32, in_sem.at[0])
    h_copy.start()
    a_copy(jnp.int32(0)).start()
    small = [
        pltpu.make_async_copy(accept_hbm, flags_raw, in_sem.at[1]),
        pltpu.make_async_copy(shrink_hbm, powers_raw, in_sem.at[2]),
        pltpu.make_async_copy(piece(w_hbm, 0, 0, 0), w_own.at[pl.ds(0, PIECE), :], in_sem.at[3]),
        pltpu.make_async_copy(piece(w_hbm, 1, 0, 0), w_own.at[pl.ds(PIECE, PIECE), :], in_sem.at[4]),
    ]
    barrier = pltpu.get_barrier_semaphore()
    peers = [at_row(d) for d in range(1, 8)] + [at_y(d) for d in range(1, 4)] + [at_z(d) for d in range(1, 4)]
    for peer in peers:
        pl.semaphore_signal(barrier, inc=1, device_id=peer, device_id_type=MESH)

    h_copy.wait()
    hi, lo = halves(h_f32[...])
    h_hi[...] = hi
    h_lo[...] = lo
    a_copy(jnp.int32(1)).start()
    for copy in small:
        copy.start()
    part = jnp.concatenate(halves(h_f32[pl.ds(pl.multiple_of(rho * 32, 32), 32), :]), axis=0)
    two = mmt(part, h_hi[...]) + mmt(part, h_lo[...])
    s1[z] = two[:32] + two[32:]

    def greeted():
        pl.semaphore_wait(barrier, len(peers))
        for d in range(1, 4):
            send(("s1", d), lambda: s1.at[z], lambda: s1.at[z], lambda d=d: at_z(d))

    def gram_y():
        for d in range(1, 4):
            arrived(("s1", d), s1.at[lax.rem(z + 4 - d, 4)], at_z(d))
        s2[y] = s1[0] + s1[1] + s1[2] + s1[3]
        for d in range(1, 4):
            send(("s2", d), lambda: s2.at[y], lambda: s2.at[y], lambda d=d: at_y(d))

    def gram_row():
        for d in range(1, 4):
            arrived(("s2", d), s2.at[lax.rem(y + 4 - d, 4)], at_y(d))
        hh_buf[rho] = s2[0] + s2[1] + s2[2] + s2[3]
        for d in range(1, 8):
            send(("s4", d), lambda: hh_buf.at[rho], lambda: hh_buf.at[rho], lambda d=d: at_row(d))

    def opposite(f):
        for d in range(2):
            for i, r in enumerate(RELAY[d]):
                send(("ra", f, d, r), lambda r=r: piece(ah, f, 2, r), lambda d=d, i=i: ra.at[f, d, i],
                     lambda d=d: step_p[f](way[d]))

    def near(f, d, r):
        send(("rb", f, d, r), lambda: piece(ah, f, way[d], r), lambda: rb.at[f, d, r], lambda: step_p[f](way[d]))

    def relayed(f, d, r):
        i = RELAY[d].index(r)
        arrived(("ra", f, d, r), ra.at[f, d, i], step_p[f](way[d]))
        at = pl.ds(row(f, way[d], r), PIECE)
        ah[at, :] += ra[f, d, i]
        near(f, d, r)

    hooks = {
        0: [greeted, lambda: opposite(0)],
        1: [lambda: opposite(1)],
        2: [lambda: near(0, 0, 3)],
        3: [lambda: near(1, 0, 3), gram_y],
        4: [lambda: near(0, 1, 2), lambda: relayed(0, 0, 2)],
        5: [lambda: near(1, 1, 2), lambda: relayed(1, 0, 2), lambda: near(0, 1, 1), lambda: relayed(0, 0, 1)],
        6: [lambda: near(1, 1, 1), lambda: relayed(1, 0, 1), lambda: relayed(0, 1, 3)],
        7: [lambda: relayed(1, 1, 3), lambda: near(0, 0, 0), lambda: near(1, 0, 0)],
    }

    @pl.loop(0, 8)
    def _(j):
        slot = lax.rem(j, 2)
        at = pl.ds(chunk_row(j), GROUP)
        a_copy(j).wait()
        hi, lo = halves(a_buf[slot])
        a_hi[at, :] = hi
        a_lo[at, :] = lo

        @pl.when(j < 6)
        def _():
            a_copy(j + 2).start()

        ah[at, :] = mmt(a_hi[at, :], h_hi[...]) + mmt(a_hi[at, :], h_lo[...]) + mmt(a_lo[at, :], h_hi[...])
        for when, steps in hooks.items():

            @pl.when(j == when)
            def _(steps=steps):
                for step in steps:
                    step()

    def own_sum(f, r):
        for d in range(2):
            arrived(("rb", f, d, r), rb.at[f, d, r], step_p[f](way[d]))
        at = pl.ds(row(f, 0, r), PIECE)
        ah[at, :] += rb[f, 0, r] + rb[f, 1, r]

    def half(f, r, start):
        return lambda: piece(ah, f, 0, r, start, 64)

    def last(f, d, part):
        start = 64 * d if part == 0 else 64 * (1 - d)
        send(("rd", f, d, part), half(f, way[d], start), lambda: rd.at[f, d, pl.ds(start, 64), :],
             lambda: step_q[f](way[d]))

    for f in range(2):
        own_sum(f, 2)
        for d in range(2):
            send(("rc", f, d), half(f, 2, 64 * d), lambda f=f, d=d: rc.at[f, d], lambda f=f, d=d: step_q[f](way[d]))

    for f in range(2):
        relayed(f, 1, 0)
    gram_row()
    for copy in small:
        copy.wait()
    acc[...] = jnp.zeros_like(acc)
    def down(line):
        return jnp.broadcast_to(line, (PIECE, PIECE)).T

    for f in range(2):
        lanes = pl.ds(row(f, 0, 0), PIECE)
        for t in range(2):
            at = slice(f * PIECE, (f + 1) * PIECE)
            flags[t, at, :] = down(flags_raw[t : t + 1, lanes].astype(F32))
            power = powers_raw[t : t + 1, lanes]
            scale = jnp.where(power == 0, 1.0, jnp.where(power == 1, 0.5, jnp.where(power == 2, 0.25, 0.125)))
            factors[t, at, :] = down(scale.astype(F32))

    for d, r in ((0, 1), (1, 3)):
        for f in range(2):
            own_sum(f, r)
            last(f, d, 1)
    for f in range(2):
        for d in range(2):
            arrived(("rc", f, d), rc.at[f, d], step_q[f](way[d]))
            at = pl.ds(pl.multiple_of(row(f, 0, way[d]) + 64 * d, 64), 64)
            ah[at, :] += rc[f, d]
            last(f, d, 0)
    for d in range(1, 8):
        arrived(("s4", d), hh_buf.at[lax.rem(rho + 8 - d, 8)], at_row(d))
    hh = hh_buf[...].reshape(RANK, RANK)
    base[...] = exact(w_own[...], hh)

    for f in range(2):
        own_sum(f, 0)
    for f in range(2):
        for d in range(2):
            for part in range(2):
                start = 64 * d if part == 0 else 64 * (1 - d)
                arrived(("rd", f, d, part), rd.at[f, d, pl.ds(start, 64), :], step_q[f](way[d]))
    own = [pl.ds(row(f, 0, 0), PIECE) for f in range(2)]
    total = jnp.concatenate([ah[own[f], :] + rd[f, 0] + rd[f, 1] for f in range(2)], axis=0)

    both = (RANK, RANK)
    eye = lax.broadcasted_iota(jnp.int32, both, 0) == lax.broadcasted_iota(jnp.int32, both, 1)
    step_size = float(RANK) / jnp.sum(jnp.where(eye, hh, 0.0), keepdims=True)

    def twice(v):
        return jnp.concatenate([v, v], axis=1)

    current = w_own[...]
    gradient = base[...] - total
    sums = []
    for t in range(2):
        change = jnp.maximum(current - twice(factors[t]) * step_size * gradient, 0.0) - current
        sums.append(jnp.sum(gradient * change, keepdims=True))
        current = current + twice(flags[t]) * change
        if t == 0:
            turned = exact(change, hh)
            sums.append(jnp.sum(change * turned, keepdims=True))
            gradient = gradient + twice(flags[t]) * turned
    for f in range(2):
        wg[own[f], :] = current[f * PIECE : (f + 1) * PIECE]

    for f in range(2):
        for d in range(2):
            send(("g1", f, d), lambda f=f: piece(wg, f, 0, 0), lambda f=f: piece(wg, f, 0, 0),
                 lambda f=f, d=d: step_q[f](way[d]))

    def spread(f, r):
        for d in range(2):
            send(("g2", f, d, r), lambda: piece(wg, f, 0, r), lambda: piece(wg, f, 0, r),
                 lambda d=d: step_p[f](way[d]))

    sums.append(jnp.sum(change * exact(change, hh), keepdims=True))
    place = lax.broadcasted_iota(jnp.int32, (8, 128), 0) * 2 + lax.broadcasted_iota(jnp.int32, (8, 128), 1)
    stats = jnp.zeros((8, 128), F32)
    for at, value in enumerate(sums):
        stats = jnp.where(place == at, value, stats)
    a1[rho] = stats
    for d in range(1, 8):
        send(("a1", d), lambda: a1.at[rho], lambda: a1.at[rho], lambda d=d: at_row(d))

    c_hi, c_lo = halves(current)
    d_hi, d_lo = halves(current.T)
    wtw[...] = mm(d_hi, c_hi) + mm(d_lo, c_hi) + mm(d_hi, c_lo)

    def rows_of(ref, k, size):
        return ref.at[pl.ds(pl.multiple_of(size * k, size), size), :]

    for d in range(1, 8):
        send(("t1", d), lambda d=d: rows_of(wtw, lax.rem(rho + d, 8), 32), lambda: t1.at[rho], lambda d=d: at_row(d))

    def factor_z():
        t1[rho] = wtw[pl.ds(pl.multiple_of(32 * rho, 32), 32), :]
        for d in range(1, 8):
            arrived(("t1", d), t1.at[lax.rem(rho + 8 - d, 8)], at_row(d))
        rows = t1[0]
        for k in range(1, 8):
            rows = rows + t1[k]
        t_sum[...] = rows
        for d in range(1, 4):
            send(("t2", d), lambda d=d: rows_of(t_sum, lax.rem(z + d, 4), 8), lambda: t2.at[z], lambda d=d: at_z(d))

    def factor_y():
        t2[z] = t_sum[pl.ds(pl.multiple_of(8 * z, 8), 8), :]
        for d in range(1, 4):
            arrived(("t2", d), t2.at[lax.rem(z + 4 - d, 4)], at_z(d))
        t3[y] = t2[0] + t2[1] + t2[2] + t2[3]
        for d in range(1, 4):
            send(("t3", d), lambda: t3.at[y], lambda: t3.at[y], lambda d=d: at_y(d))

    def factor_all():
        for d in range(1, 4):
            arrived(("t3", d), t3.at[lax.rem(y + 4 - d, 4)], at_y(d))
        t_all[pl.ds(pl.multiple_of(8 * z, 8), 8), :] = t3[0] + t3[1] + t3[2] + t3[3]
        for d in range(1, 4):
            send(("t4", d), lambda: rows_of(t_all, z, 8), lambda: rows_of(t_all, z, 8), lambda d=d: at_z(d))

    def stats_y():
        for d in range(1, 8):
            arrived(("a1", d), a1.at[lax.rem(rho + 8 - d, 8)], at_row(d))
        a2[y] = sum(a1[k] for k in range(1, 8)) + a1[0]
        for d in range(1, 4):
            send(("a2", d), lambda: a2.at[y], lambda: a2.at[y], lambda d=d: at_y(d))

    def stats_z():
        for d in range(1, 4):
            arrived(("a2", d), a2.at[lax.rem(y + 4 - d, 4)], at_y(d))
        a3[z] = a2[0] + a2[1] + a2[2] + a2[3]
        for d in range(1, 4):
            send(("a3", d), lambda: a3.at[z], lambda: a3.at[z], lambda d=d: at_z(d))

    def beside(f):
        for d in range(2):
            r = 4 - way[d]
            arrived(("g1", f, d), piece(wg, f, 0, r), step_q[f](way[d]))
            send(("g1h", f, d), lambda r=r, d=d: piece(wg, f, 0, r, 64 * d, 64),
                 lambda r=r, d=d: piece(wg, f, 0, r, 64 * d, 64), lambda d=d: step_q[f](way[d]))

    def across_ring(f):
        for d in range(2):
            arrived(("g1h", f, d), piece(wg, f, 0, 2, 64 * d, 64), step_q[f](way[d]))
        spread(f, 2)

    def onward(f, r):
        for d in range(2):
            dp = 4 - way[d]
            arrived(("g2", f, d, r), piece(wg, f, dp, r), step_p[f](way[d]))
            send(("g2h", f, d, r), lambda dp=dp, d=d: piece(wg, f, dp, r, 64 * d, 64),
                 lambda dp=dp, d=d: piece(wg, f, dp, r, 64 * d, 64), lambda d=d: step_p[f](way[d]))

    def far(f, r):
        for d in range(2):
            arrived(("g2h", f, d, r), piece(wg, f, 2, r, 64 * d, 64), step_p[f](way[d]))

    def pair(step, *given):
        return lambda: [step(f, *given) for f in range(2)]

    before = {
        1: [pair(spread, 0), pair(beside)],
        2: [pair(spread, 1)],
        3: [pair(onward, 0)],
        4: [pair(spread, 3), stats_y, factor_z],
        5: [pair(across_ring)],
        6: [pair(onward, 1)],
        8: [pair(far, 0)],
        9: [pair(onward, 3), stats_z, factor_y],
        11: [pair(far, 1)],
        12: [pair(onward, 2)],
        14: [pair(far, 3), factor_all],
    }
    order = ((0, 0), (0, 1), (0, 3), (1, 0), (3, 0), (0, 2), (1, 1), (3, 1),
             (2, 0), (1, 3), (3, 3), (2, 1), (1, 2), (3, 2), (2, 3), (2, 2))
    codes = tuple(jnp.int32(sum((pair_[i] + 2) % 4 * 4**u for u, pair_ in enumerate(order))) for i in range(2))

    def factor_halves(at):
        return halves(jnp.concatenate([wg[at[0], :], wg[at[1], :]], axis=0).T)

    def gather(at, left, t):
        cols = slice(t * WIDTH, (t + 1) * WIDTH)
        m_hi = jnp.concatenate([a_hi[at[0], cols], a_hi[at[1], cols]], axis=0)
        m_lo = jnp.concatenate([a_lo[at[0], cols], a_lo[at[1], cols]], axis=0)
        acc[t] = acc[t] + mm(left[0], m_hi) + mm(left[1], m_hi) + mm(left[0], m_lo)

    def unit(u, codes):
        for when, steps in before.items():

            @pl.when(u == when)
            def _(steps=steps):
                for step in steps:
                    step()

        dp, r = lax.rem(codes[0], 4) + 2, lax.rem(codes[1], 4) + 2
        at = [pl.ds(row(f, dp, r), PIECE) for f in range(2)]

        left = factor_halves(at)
        for t in range(TILES):
            gather(at, left, t)
        return lax.div(codes[0], 4), lax.div(codes[1], 4)

    lax.fori_loop(0, 15, unit, codes)

    def block(t, k, mine, start=0, size=32):
        at = 64 * lax.rem(x + k, 4) + 32 * (core if mine else 1 - core) + start
        return (t, pl.ds(pl.multiple_of(at, 16), size), slice(None))

    def to_partner(t):
        for k in (2, 1, 3, 0):
            send(("core", t, k), lambda k=k: acc.at[block(t, k, False)], lambda k=k: core_in.at[t, k], lambda: partner)

    def joined(t, k):
        arrived(("core", t, k), core_in.at[t, k], partner)
        acc[block(t, k, True)] += core_in[t, k]

    def first(t):
        joined(t, 2)
        for d in range(2):
            send(("ga", t, d), lambda d=d: acc.at[block(t, 2, True, 16 * d, 16)], lambda d=d: ga.at[t, d],
                 lambda d=d: at_x(way[d]))

    def beyond(t):
        for d in range(2):
            joined(t, way[d])
            onto(t, d, 1)
        joined(t, 0)

    def onto(t, d, part):
        start = 16 * d if part == 0 else 16 * (1 - d)
        send(("gb", t, d, part), lambda: acc.at[block(t, way[d], True, start, 16)],
             lambda: gb.at[t, d, pl.ds(start, 16), :], lambda: at_x(way[d]))

    def second(t):
        for d in range(2):
            arrived(("ga", t, d), ga.at[t, d], at_x(way[d]))
            acc[block(t, way[d], True, 16 * d, 16)] += ga[t, d]
            onto(t, d, 0)

    def third(t):
        for d in range(2):
            for part in range(2):
                start = 16 * d if part == 0 else 16 * (1 - d)
                arrived(("gb", t, d, part), gb.at[t, d, pl.ds(start, 16), :], at_x(way[d]))
        g_out[:, t * WIDTH : (t + 1) * WIDTH] -= acc[block(t, 0, True)] + gb[t, 0] + gb[t, 1]

    def leave(items):
        for key, src, dst, to in items:
            make(key, src(), dst(), to()).wait_send()

    before_tail = list(sent)
    for f in range(2):
        far(f, 2)
    at = [pl.ds(row(f, 2, 2), PIECE) for f in range(2)]
    left = factor_halves(at)
    for t in range(TILES):
        gather(at, left, t)
        to_partner(t)
        if t > 0:
            first(t - 1)
    first(TILES - 1)
    for t in range(TILES):
        beyond(t)
    for d in range(1, 4):
        arrived(("t4", d), rows_of(t_all, lax.rem(z + 4 - d, 4), 8), at_z(d))
    t_hi, t_lo = halves(t_all[...])
    for t in range(TILES):
        cols = slice(t * WIDTH, (t + 1) * WIDTH)
        g_out[:, cols] = mm(t_hi, h_hi[:, cols]) + mm(t_hi, h_lo[:, cols]) + mm(t_lo, h_hi[:, cols])
    leave(before_tail)
    for t in range(TILES):
        second(t)
    for d in range(1, 4):
        arrived(("a3", d), a3.at[lax.rem(z + 4 - d, 4)], at_z(d))
    stat_out[...] = (a3[0] + a3[1] + a3[2] + a3[3])[:2, :2]
    for t in range(TILES):
        third(t)
    leave(sent[len(before_tail) :])


def per_device(a_matrix, h_factor, w_factor, accept, shrink):
    vmem = pltpu.VMEM
    anywhere = pl.BlockSpec(memory_space=pl.ANY)
    inside = pl.BlockSpec(memory_space=vmem)
    return pl.pallas_call(
        kernel,
        out_shape=(
            vmem((ROWS, RANK), F32),
            vmem((RANK // 8, COLS), F32),
            vmem((2, 2), F32),
        ),
        in_specs=[anywhere] * 5,
        out_specs=(inside, inside, inside),
        scratch_shapes=[
            vmem((2, GROUP, COLS), F32),
            vmem((ROWS, COLS), BF16),
            vmem((ROWS, COLS), BF16),
            vmem((RANK, COLS), F32),
            vmem((RANK, COLS), BF16),
            vmem((RANK, COLS), BF16),
            vmem((ROWS, RANK), F32),
            vmem((2, 2, 2, PIECE, RANK), F32),
            vmem((2, 2, 4, PIECE, RANK), F32),
            vmem((2, 2, 64, RANK), F32),
            vmem((2, 2, PIECE, RANK), F32),
            vmem((4, 32, RANK), F32),
            vmem((4, 32, RANK), F32),
            vmem((8, 32, RANK), F32),
            vmem((32, RANK), F32),
            vmem((4, 8, RANK), F32),
            vmem((4, 8, RANK), F32),
            vmem((32, RANK), F32),
            vmem((8, 32, RANK), F32),
            vmem((RANK, RANK), F32),
            vmem((2, ROWS), jnp.int32),
            vmem((2, ROWS), jnp.int32),
            vmem((2, RANK, PIECE), F32),
            vmem((2, RANK, PIECE), F32),
            vmem((RANK, RANK), F32),
            vmem((TILES, RANK, WIDTH), F32),
            vmem((RANK, RANK), F32),
            vmem((TILES, 4, 32, WIDTH), F32),
            vmem((TILES, 2, 16, WIDTH), F32),
            vmem((TILES, 2, 32, WIDTH), F32),
            vmem((8, 8, 128), F32),
            vmem((4, 8, 128), F32),
            vmem((4, 8, 128), F32),
            pltpu.SemaphoreType.DMA((len(KEYS),)),
            pltpu.SemaphoreType.DMA((len(KEYS),)),
            pltpu.SemaphoreType.DMA((2,)),
            pltpu.SemaphoreType.DMA((5,)),
        ],
        compiler_params=pltpu.CompilerParams(
            collective_id=0, has_side_effects=True, vmem_limit_bytes=58 * 1024 * 1024
        ),
    )(a_matrix, h_factor, w_factor, accept.T, shrink.T)

def solution(mesh):
    in_specs = (P("row", "col"), P(None, "col"), P("row", None), P("row", None), P("row", None))
    out_specs = (P("row", None), P("row", "col"), P())
    return jax.shard_map(per_device, mesh=mesh, in_specs=in_specs, out_specs=out_specs, check_vma=False)
```

```python
import functools

import jax
import jax.numpy as jnp
from jax import lax
from jax.experimental import pallas as pl
from jax.experimental.pallas import tpu as pltpu
from jax.sharding import PartitionSpec as P

F32, BF16 = jnp.float32, jnp.bfloat16
MESH = pl.DeviceIdType.MESH
RANK, ROWS, COLS = 256, 4096, 1536
PIECE, GROUP, FLOW = 128, 512, 2048
TILES = 3
WIDTH = COLS // TILES
RELAY = (((2, 1), (3, 0)))


def halves(x):
    hi = x.astype(BF16)
    return hi, (x - hi.astype(F32)).astype(BF16)


def mm(a, b):
    return lax.dot_general(a, b, (((1,), (0,)), ((), ())), preferred_element_type=F32)


def mmt(a, b):
    return lax.dot_general(a, b, (((1,), (1,)), ((), ())), preferred_element_type=F32)


def exact(a, b):
    return jnp.dot(a, b, precision=lax.Precision.HIGHEST, preferred_element_type=F32)


def sem_keys():
    keys = []
    for f in range(2):
        for d in range(2):
            keys += [("ra", f, d, r) for r in RELAY[d]]
            keys += [("rb", f, d, r) for r in range(4)]
            keys += [("rc", f, d), ("rd", f, d, 0), ("rd", f, d, 1)]
            keys += [("g1", f, d), ("g1h", f, d)]
            keys += [("g2", f, d, r) for r in range(4)]
            keys += [("g2h", f, d, r) for r in range(4)]
    for name, count in (("s1", 4), ("s2", 4), ("s4", 8), ("t1", 8), ("t2", 4), ("t3", 4), ("t4", 4), ("a1", 8), ("a2", 4), ("a3", 4)):
        keys += [(name, d) for d in range(1, count)]
    for t in range(TILES):
        keys += [("core", t, k) for k in range(4)]
        for d in range(2):
            keys += [("ga", t, d), ("gb", t, d, 0), ("gb", t, d, 1)]
    return {key: at for at, key in enumerate(keys)}


KEYS = sem_keys()


def kernel(
    a_hbm, h_hbm, w_hbm, accept_hbm, shrink_hbm,
    wg, g_out, stat_out,
    a_buf, a_hi, a_lo, h_f32, h_hi, h_lo,
    ah, ra, rb, rc, rd,
    s1, s2, t1, t_sum, t2, t3, t_all, hh_buf,
    w_own, flags_raw, powers_raw, flags, factors, base, updated,
    acc, wtw, core_in, ga, gb, a1, a2, a3,
    send_sem, recv_sem, a_sem, in_sem,
):
    rho, col = lax.axis_index("row"), lax.axis_index("col")
    y, z = lax.div(col, 4), lax.rem(col, 4)
    x, core = lax.div(rho, 2), lax.rem(rho, 2)
    along, across = (y, z), (z, y)

    def at_y(d):
        return (rho, lax.rem(y + d, 4) * 4 + z)

    def at_z(d):
        return (rho, y * 4 + lax.rem(z + d, 4))

    def at_row(d):
        return (lax.rem(rho + d, 8), col)

    def at_x(d):
        return (lax.rem(x + d, 4) * 2 + core, col)

    partner = (x * 2 + 1 - core, col)
    step_p, step_q = (at_y, at_z), (at_z, at_y)
    way = (1, 3)

    def row(f, dp, dq):
        return pl.multiple_of(
            f * FLOW + GROUP * lax.rem(along[f] + dp, 4) + PIECE * lax.rem(across[f] + dq, 4), PIECE
        )

    def piece(ref, f, dp, dq, start=0, size=PIECE):
        return ref.at[pl.ds(pl.multiple_of(row(f, dp, dq) + start, 64), size), :]

    sent = []

    def make(key, src, dst, to):
        return pltpu.make_async_remote_copy(
            src_ref=src, dst_ref=dst, send_sem=send_sem.at[KEYS[key]], recv_sem=recv_sem.at[KEYS[key]],
            device_id=to, device_id_type=MESH,
        )

    def send(key, src, dst, to):
        make(key, src(), dst(), to()).start()
        sent.append((key, src, dst, to))

    def arrived(key, dst, to):
        make(key, dst, dst, to).wait_recv()

    def chunk_row(j):
        f, t = lax.rem(j, 2), lax.div(j, 2)
        dp = 2 - t + 3 * lax.div(t, 2) - 2 * lax.div(t, 3)
        return pl.multiple_of(f * FLOW + GROUP * lax.rem(y + f * (z - y) + dp, 4), GROUP)

    def a_copy(j):
        slot = lax.rem(j, 2)
        return pltpu.make_async_copy(a_hbm.at[pl.ds(chunk_row(j), GROUP), :], a_buf.at[slot], a_sem.at[slot])

    h_copy = pltpu.make_async_copy(h_hbm, h_f32, in_sem.at[0])
    h_copy.start()
    a_copy(jnp.int32(0)).start()
    small = [
        pltpu.make_async_copy(accept_hbm, flags_raw, in_sem.at[1]),
        pltpu.make_async_copy(shrink_hbm, powers_raw, in_sem.at[2]),
        pltpu.make_async_copy(piece(w_hbm, 0, 0, 0), w_own.at[pl.ds(0, PIECE), :], in_sem.at[3]),
        pltpu.make_async_copy(piece(w_hbm, 1, 0, 0), w_own.at[pl.ds(PIECE, PIECE), :], in_sem.at[4]),
    ]
    barrier = pltpu.get_barrier_semaphore()
    peers = [at_row(d) for d in range(1, 8)] + [at_y(d) for d in range(1, 4)] + [at_z(d) for d in range(1, 4)]
    for peer in peers:
        pl.semaphore_signal(barrier, inc=1, device_id=peer, device_id_type=MESH)

    h_copy.wait()
    hi, lo = halves(h_f32[...])
    h_hi[...] = hi
    h_lo[...] = lo
    a_copy(jnp.int32(1)).start()
    for copy in small:
        copy.start()
    part = jnp.concatenate(halves(h_f32[pl.ds(pl.multiple_of(rho * 32, 32), 32), :]), axis=0)
    two = mmt(part, h_hi[...]) + mmt(part, h_lo[...])
    s1[z] = two[:32] + two[32:]

    def greeted():
        pl.semaphore_wait(barrier, len(peers))
        for d in range(1, 4):
            send(("s1", d), lambda: s1.at[z], lambda: s1.at[z], lambda d=d: at_z(d))

    def gram_y():
        for d in range(1, 4):
            arrived(("s1", d), s1.at[lax.rem(z + 4 - d, 4)], at_z(d))
        s2[y] = s1[0] + s1[1] + s1[2] + s1[3]
        for d in range(1, 4):
            send(("s2", d), lambda: s2.at[y], lambda: s2.at[y], lambda d=d: at_y(d))

    def gram_row():
        for d in range(1, 4):
            arrived(("s2", d), s2.at[lax.rem(y + 4 - d, 4)], at_y(d))
        hh_buf[rho] = s2[0] + s2[1] + s2[2] + s2[3]
        for d in range(1, 8):
            send(("s4", d), lambda: hh_buf.at[rho], lambda: hh_buf.at[rho], lambda d=d: at_row(d))

    def opposite(f):
        for d in range(2):
            for i, r in enumerate(RELAY[d]):
                send(("ra", f, d, r), lambda r=r: piece(ah, f, 2, r), lambda d=d, i=i: ra.at[f, d, i],
                     lambda d=d: step_p[f](way[d]))

    def near(f, d, r):
        send(("rb", f, d, r), lambda: piece(ah, f, way[d], r), lambda: rb.at[f, d, r], lambda: step_p[f](way[d]))

    def relayed(f, d, r):
        i = RELAY[d].index(r)
        arrived(("ra", f, d, r), ra.at[f, d, i], step_p[f](way[d]))
        at = pl.ds(row(f, way[d], r), PIECE)
        ah[at, :] += ra[f, d, i]
        near(f, d, r)

    hooks = {
        0: [greeted, lambda: opposite(0)],
        1: [lambda: opposite(1)],
        2: [lambda: near(0, 0, 3)],
        3: [lambda: near(1, 0, 3)],
        4: [lambda: near(0, 1, 2), lambda: relayed(0, 0, 2), gram_y],
        5: [lambda: near(1, 1, 2), lambda: relayed(1, 0, 2), lambda: near(0, 1, 1), lambda: relayed(0, 0, 1)],
        6: [lambda: near(1, 1, 1), lambda: relayed(1, 0, 1), lambda: relayed(0, 1, 3)],
        7: [lambda: relayed(1, 1, 3)],
    }

    @pl.loop(0, 8)
    def _(j):
        slot = lax.rem(j, 2)
        at = pl.ds(chunk_row(j), GROUP)
        a_copy(j).wait()
        hi, lo = halves(a_buf[slot])
        a_hi[at, :] = hi
        a_lo[at, :] = lo

        @pl.when(j < 6)
        def _():
            a_copy(j + 2).start()

        ah[at, :] = mmt(a_hi[at, :], h_hi[...]) + mmt(a_hi[at, :], h_lo[...]) + mmt(a_lo[at, :], h_hi[...])
        for when, steps in hooks.items():

            @pl.when(j == when)
            def _(steps=steps):
                for step in steps:
                    step()

    def own_sum(f, r):
        for d in range(2):
            arrived(("rb", f, d, r), rb.at[f, d, r], step_p[f](way[d]))
        at = pl.ds(row(f, 0, r), PIECE)
        ah[at, :] += rb[f, 0, r] + rb[f, 1, r]

    def half(f, r, start):
        return lambda: piece(ah, f, 0, r, start, 64)

    def last(f, d, part):
        start = 64 * d if part == 0 else 64 * (1 - d)
        send(("rd", f, d, part), half(f, way[d], start), lambda: rd.at[f, d, pl.ds(start, 64), :],
             lambda: step_q[f](way[d]))

    for f in range(2):
        own_sum(f, 2)
        for d in range(2):
            send(("rc", f, d), half(f, 2, 64 * d), lambda f=f, d=d: rc.at[f, d], lambda f=f, d=d: step_q[f](way[d]))

    for f in range(2):
        near(f, 0, 0)
        relayed(f, 1, 0)
    gram_row()
    for copy in small:
        copy.wait()
    acc[...] = jnp.zeros_like(acc)
    def down(line):
        return jnp.broadcast_to(line, (PIECE, PIECE)).T

    for f in range(2):
        lanes = pl.ds(row(f, 0, 0), PIECE)
        for t in range(2):
            at = slice(f * PIECE, (f + 1) * PIECE)
            flags[t, at, :] = down(flags_raw[t : t + 1, lanes].astype(F32))
            power = powers_raw[t : t + 1, lanes]
            scale = jnp.where(power == 0, 1.0, jnp.where(power == 1, 0.5, jnp.where(power == 2, 0.25, 0.125)))
            factors[t, at, :] = down(scale.astype(F32))

    for d, r in ((0, 1), (1, 3)):
        for f in range(2):
            own_sum(f, r)
            last(f, d, 1)
    for f in range(2):
        for d in range(2):
            arrived(("rc", f, d), rc.at[f, d], step_q[f](way[d]))
            at = pl.ds(pl.multiple_of(row(f, 0, way[d]) + 64 * d, 64), 64)
            ah[at, :] += rc[f, d]
            last(f, d, 0)
    for d in range(1, 8):
        arrived(("s4", d), hh_buf.at[lax.rem(rho + 8 - d, 8)], at_row(d))
    hh = hh_buf[...].reshape(RANK, RANK)
    base[...] = exact(w_own[...], hh)

    for f in range(2):
        own_sum(f, 0)
    own = [pl.ds(row(f, 0, 0), PIECE) for f in range(2)]

    both = (RANK, RANK)
    eye = lax.broadcasted_iota(jnp.int32, both, 0) == lax.broadcasted_iota(jnp.int32, both, 1)
    step_size = float(RANK) / jnp.sum(jnp.where(eye, hh, 0.0), keepdims=True)

    def twice(v):
        return jnp.concatenate([v, v], axis=1)

    def trials(f):
        for d in range(2):
            for part in range(2):
                start = 64 * d if part == 0 else 64 * (1 - d)
                arrived(("rd", f, d, part), rd.at[f, d, pl.ds(start, 64), :], step_q[f](way[d]))
        at = slice(f * PIECE, (f + 1) * PIECE)
        current = w_own[at, :]
        gradient = base[at, :] - (ah[own[f], :] + rd[f, 0] + rd[f, 1])
        sums = []
        for t in range(2):
            change = jnp.maximum(current - twice(factors[t, at, :]) * step_size * gradient, 0.0) - current
            sums.append(jnp.sum(gradient * change, keepdims=True))
            current = current + twice(flags[t, at, :]) * change
            if t == 0:
                turned = exact(change, hh)
                sums.append(jnp.sum(change * turned, keepdims=True))
                gradient = gradient + twice(flags[t, at, :]) * turned
        wg[own[f], :] = current
        for d in range(2):
            send(("g1", f, d), lambda: piece(wg, f, 0, 0), lambda: piece(wg, f, 0, 0),
                 lambda d=d: step_q[f](way[d]))
        updated[at, :] = current
        return sums, change

    def spread(f, r):
        for d in range(2):
            send(("g2", f, d, r), lambda: piece(wg, f, 0, r), lambda: piece(wg, f, 0, r),
                 lambda d=d: step_p[f](way[d]))

    made = [trials(0), trials(1)]
    spread(0, 0)
    ends = jnp.concatenate([change for _, change in made], axis=0)
    sums = [first_ + second_ for first_, second_ in zip(made[0][0], made[1][0])]
    sums.append(jnp.sum(ends * exact(ends, hh), keepdims=True))
    place = lax.broadcasted_iota(jnp.int32, (8, 128), 0) * 2 + lax.broadcasted_iota(jnp.int32, (8, 128), 1)
    stats = jnp.zeros((8, 128), F32)
    for at, value in enumerate(sums):
        stats = jnp.where(place == at, value, stats)
    a1[rho] = stats
    for d in range(1, 8):
        send(("a1", d), lambda: a1.at[rho], lambda: a1.at[rho], lambda d=d: at_row(d))

    current = updated[...]
    c_hi, c_lo = halves(current)
    d_hi, d_lo = halves(current.T)
    wtw[...] = mm(d_hi, c_hi) + mm(d_lo, c_hi) + mm(d_hi, c_lo)

    def rows_of(ref, k, size):
        return ref.at[pl.ds(pl.multiple_of(size * k, size), size), :]

    for d in range(1, 8):
        send(("t1", d), lambda d=d: rows_of(wtw, lax.rem(rho + d, 8), 32), lambda: t1.at[rho], lambda d=d: at_row(d))

    def factor_z():
        t1[rho] = wtw[pl.ds(pl.multiple_of(32 * rho, 32), 32), :]
        for d in range(1, 8):
            arrived(("t1", d), t1.at[lax.rem(rho + 8 - d, 8)], at_row(d))
        rows = t1[0]
        for k in range(1, 8):
            rows = rows + t1[k]
        t_sum[...] = rows
        for d in range(1, 4):
            send(("t2", d), lambda d=d: rows_of(t_sum, lax.rem(z + d, 4), 8), lambda: t2.at[z], lambda d=d: at_z(d))

    def factor_y():
        t2[z] = t_sum[pl.ds(pl.multiple_of(8 * z, 8), 8), :]
        for d in range(1, 4):
            arrived(("t2", d), t2.at[lax.rem(z + 4 - d, 4)], at_z(d))
        t3[y] = t2[0] + t2[1] + t2[2] + t2[3]
        for d in range(1, 4):
            send(("t3", d), lambda: t3.at[y], lambda: t3.at[y], lambda d=d: at_y(d))

    def factor_all():
        for d in range(1, 4):
            arrived(("t3", d), t3.at[lax.rem(y + 4 - d, 4)], at_y(d))
        t_all[pl.ds(pl.multiple_of(8 * z, 8), 8), :] = t3[0] + t3[1] + t3[2] + t3[3]
        for d in range(1, 4):
            send(("t4", d), lambda: rows_of(t_all, z, 8), lambda: rows_of(t_all, z, 8), lambda d=d: at_z(d))

    def stats_y():
        for d in range(1, 8):
            arrived(("a1", d), a1.at[lax.rem(rho + 8 - d, 8)], at_row(d))
        a2[y] = sum(a1[k] for k in range(1, 8)) + a1[0]
        for d in range(1, 4):
            send(("a2", d), lambda: a2.at[y], lambda: a2.at[y], lambda d=d: at_y(d))

    def stats_z():
        for d in range(1, 4):
            arrived(("a2", d), a2.at[lax.rem(y + 4 - d, 4)], at_y(d))
        a3[z] = a2[0] + a2[1] + a2[2] + a2[3]
        for d in range(1, 4):
            send(("a3", d), lambda: a3.at[z], lambda: a3.at[z], lambda d=d: at_z(d))

    def beside(f):
        for d in range(2):
            r = 4 - way[d]
            arrived(("g1", f, d), piece(wg, f, 0, r), step_q[f](way[d]))
            send(("g1h", f, d), lambda r=r, d=d: piece(wg, f, 0, r, 64 * d, 64),
                 lambda r=r, d=d: piece(wg, f, 0, r, 64 * d, 64), lambda d=d: step_q[f](way[d]))

    def across_ring(f):
        for d in range(2):
            arrived(("g1h", f, d), piece(wg, f, 0, 2, 64 * d, 64), step_q[f](way[d]))
        spread(f, 2)

    def come(f, r):
        for d in range(2):
            arrived(("g2", f, d, r), piece(wg, f, 4 - way[d], r), step_p[f](way[d]))

    def onward(f, r):
        for d in range(2):
            dp = 4 - way[d]
            send(("g2h", f, d, r), lambda dp=dp, d=d: piece(wg, f, dp, r, 64 * d, 64),
                 lambda dp=dp, d=d: piece(wg, f, dp, r, 64 * d, 64), lambda d=d: step_p[f](way[d]))

    def far(f, r):
        for d in range(2):
            arrived(("g2h", f, d, r), piece(wg, f, 2, r, 64 * d, 64), step_p[f](way[d]))

    def pair(step, *given):
        return lambda: [step(f, *given) for f in range(2)]

    before = {
        0: [lambda: spread(1, 0), pair(beside), pair(spread, 1), pair(spread, 3)],
        1: [pair(come, 0)],
        2: [pair(across_ring), stats_y, factor_z, pair(onward, 0)],
        3: [pair(come, 1), pair(onward, 1)],
        4: [pair(come, 3), pair(onward, 3)],
        5: [pair(come, 2), pair(onward, 2), stats_z, factor_y],
        6: [pair(far, 0), pair(far, 1)],
        7: [pair(far, 3), pair(far, 2)],
    }
    order = (((0, 0), (0, 1)), ((1, 0), (3, 0)), ((0, 3), (0, 2)), ((1, 1), (3, 1)),
             ((1, 3), (3, 3)), ((1, 2), (3, 2)), ((2, 0), (2, 1)), ((2, 3), (2, 2)))
    codes = tuple(
        jnp.int32(sum(cell[n][i] * 4**u for u, cell in enumerate(order))) for n in range(2) for i in range(2)
    )

    def factor_halves(at):
        return halves(jnp.concatenate([wg[rows, :] for rows in at], axis=0).T)

    def block(t, k, mine, start=0, size=32):
        at = 64 * lax.rem(x + k, 4) + 32 * (core if mine else 1 - core) + start
        return (t, pl.ds(pl.multiple_of(at, 16), size), slice(None))

    def to_partner(t):
        for k in (2, 1, 3, 0):
            send(("core", t, k), lambda k=k: acc.at[block(t, k, False)], lambda k=k: core_in.at[t, k], lambda: partner)

    def unit(u, codes):
        for when, steps in before.items():

            @pl.when(u == when)
            def _(steps=steps):
                for step in steps:
                    step()

        at = []
        for n in range(2):
            dp, r = lax.rem(codes[2 * n], 4), lax.rem(codes[2 * n + 1], 4)
            at += [pl.ds(row(f, dp, r), PIECE) for f in range(2)]
        left_hi, left_lo = factor_halves(at)
        for t in range(TILES):
            cols = slice(t * WIDTH, (t + 1) * WIDTH)
            m_hi = jnp.concatenate([a_hi[rows, cols] for rows in at], axis=0)
            m_lo = jnp.concatenate([a_lo[rows, cols] for rows in at], axis=0)
            acc[t] = acc[t] + mm(left_hi, m_hi) + mm(left_lo, m_hi) + mm(left_hi, m_lo)
        return tuple(lax.div(code, 4) for code in codes)

    lax.fori_loop(0, 8, unit, codes)

    def joined(t, k):
        arrived(("core", t, k), core_in.at[t, k], partner)
        acc[block(t, k, True)] += core_in[t, k]

    def first(t):
        joined(t, 2)
        for d in range(2):
            send(("ga", t, d), lambda d=d: acc.at[block(t, 2, True, 16 * d, 16)], lambda d=d: ga.at[t, d],
                 lambda d=d: at_x(way[d]))

    def beyond(t):
        for d in range(2):
            joined(t, way[d])
            onto(t, d, 1)
        joined(t, 0)

    def onto(t, d, part):
        start = 16 * d if part == 0 else 16 * (1 - d)
        send(("gb", t, d, part), lambda: acc.at[block(t, way[d], True, start, 16)],
             lambda: gb.at[t, d, pl.ds(start, 16), :], lambda: at_x(way[d]))

    def second(t):
        for d in range(2):
            arrived(("ga", t, d), ga.at[t, d], at_x(way[d]))
            acc[block(t, way[d], True, 16 * d, 16)] += ga[t, d]
            onto(t, d, 0)

    def third(t):
        for d in range(2):
            for part in range(2):
                start = 16 * d if part == 0 else 16 * (1 - d)
                arrived(("gb", t, d, part), gb.at[t, d, pl.ds(start, 16), :], at_x(way[d]))
        g_out[:, t * WIDTH : (t + 1) * WIDTH] -= acc[block(t, 0, True)] + gb[t, 0] + gb[t, 1]

    def leave(items):
        for key, src, dst, to in items:
            make(key, src(), dst(), to()).wait_send()

    before_tail = list(sent)
    for t in range(TILES):
        to_partner(t)
    for t in range(TILES):
        first(t)
    for t in range(TILES):
        beyond(t)
    factor_all()
    for t in range(TILES):
        second(t)
    leave(before_tail)
    for d in range(1, 4):
        arrived(("t4", d), rows_of(t_all, lax.rem(z + 4 - d, 4), 8), at_z(d))
    t_hi, t_lo = halves(t_all[...])
    for t in range(TILES):
        cols = slice(t * WIDTH, (t + 1) * WIDTH)
        g_out[:, cols] = mm(t_hi, h_hi[:, cols]) + mm(t_hi, h_lo[:, cols]) + mm(t_lo, h_hi[:, cols])
    for d in range(1, 4):
        arrived(("a3", d), a3.at[lax.rem(z + 4 - d, 4)], at_z(d))
    stat_out[...] = (a3[0] + a3[1] + a3[2] + a3[3])[:2, :2]
    for t in range(TILES):
        third(t)
    leave(sent[len(before_tail) :])


def per_device(a_matrix, h_factor, w_factor, accept, shrink):
    vmem = pltpu.VMEM
    anywhere = pl.BlockSpec(memory_space=pl.ANY)
    inside = pl.BlockSpec(memory_space=vmem)
    return pl.pallas_call(
        kernel,
        out_shape=(
            vmem((ROWS, RANK), F32),
            vmem((RANK // 8, COLS), F32),
            vmem((2, 2), F32),
        ),
        in_specs=[anywhere] * 5,
        out_specs=(inside, inside, inside),
        scratch_shapes=[
            vmem((2, GROUP, COLS), F32),
            vmem((ROWS, COLS), BF16),
            vmem((ROWS, COLS), BF16),
            vmem((RANK, COLS), F32),
            vmem((RANK, COLS), BF16),
            vmem((RANK, COLS), BF16),
            vmem((ROWS, RANK), F32),
            vmem((2, 2, 2, PIECE, RANK), F32),
            vmem((2, 2, 4, PIECE, RANK), F32),
            vmem((2, 2, 64, RANK), F32),
            vmem((2, 2, PIECE, RANK), F32),
            vmem((4, 32, RANK), F32),
            vmem((4, 32, RANK), F32),
            vmem((8, 32, RANK), F32),
            vmem((32, RANK), F32),
            vmem((4, 8, RANK), F32),
            vmem((4, 8, RANK), F32),
            vmem((32, RANK), F32),
            vmem((8, 32, RANK), F32),
            vmem((RANK, RANK), F32),
            vmem((2, ROWS), jnp.int32),
            vmem((2, ROWS), jnp.int32),
            vmem((2, RANK, PIECE), F32),
            vmem((2, RANK, PIECE), F32),
            vmem((RANK, RANK), F32),
            vmem((RANK, RANK), F32),
            vmem((TILES, RANK, WIDTH), F32),
            vmem((RANK, RANK), F32),
            vmem((TILES, 4, 32, WIDTH), F32),
            vmem((TILES, 2, 16, WIDTH), F32),
            vmem((TILES, 2, 32, WIDTH), F32),
            vmem((8, 8, 128), F32),
            vmem((4, 8, 128), F32),
            vmem((4, 8, 128), F32),
            pltpu.SemaphoreType.DMA((len(KEYS),)),
            pltpu.SemaphoreType.DMA((len(KEYS),)),
            pltpu.SemaphoreType.DMA((2,)),
            pltpu.SemaphoreType.DMA((5,)),
        ],
        compiler_params=pltpu.CompilerParams(
            collective_id=0, has_side_effects=True, vmem_limit_bytes=58 * 1024 * 1024
        ),
    )(a_matrix, h_factor, w_factor, accept.T, shrink.T)

def solution(mesh):
    in_specs = (P("row", "col"), P(None, "col"), P("row", None), P("row", None), P("row", None))
    out_specs = (P("row", None), P("row", "col"), P())
    return jax.shard_map(per_device, mesh=mesh, in_specs=in_specs, out_specs=out_specs, check_vma=False)
```

```python
import functools

import jax
import jax.numpy as jnp
from jax import lax
from jax.experimental import pallas as pl
from jax.experimental.pallas import tpu as pltpu
from jax.sharding import PartitionSpec as P

F32, BF16 = jnp.float32, jnp.bfloat16
MESH = pl.DeviceIdType.MESH
RANK, ROWS, COLS = 256, 4096, 1536
PIECE, GROUP, FLOW = 128, 512, 2048
TILES = 3
WIDTH = COLS // TILES
RELAY = (((2, 1), (3, 0)))


def halves(x):
    hi = x.astype(BF16)
    return hi, (x - hi.astype(F32)).astype(BF16)


def mm(a, b):
    return lax.dot_general(a, b, (((1,), (0,)), ((), ())), preferred_element_type=F32)


def mmt(a, b):
    return lax.dot_general(a, b, (((1,), (1,)), ((), ())), preferred_element_type=F32)


def exact(a, b):
    return jnp.dot(a, b, precision=lax.Precision.HIGHEST, preferred_element_type=F32)


def sem_keys():
    keys = []
    for f in range(2):
        for d in range(2):
            keys += [("ra", f, d, r) for r in RELAY[d]]
            keys += [("rb", f, d, r) for r in range(4)]
            keys += [("rc", f, d), ("rd", f, d, 0), ("rd", f, d, 1)]
            keys += [("g1", f, d), ("g1h", f, d)]
            keys += [("g2", f, d, r) for r in range(4)]
            keys += [("g2h", f, d, r) for r in range(4)]
    for name, count in (("s1", 4), ("s2", 4), ("s4", 8), ("t1", 8), ("t2", 4), ("t3", 4), ("t4", 4), ("a1", 8), ("a2", 4), ("a3", 4)):
        keys += [(name, d) for d in range(1, count)]
    for t in range(TILES):
        keys += [("core", t, k) for k in range(4)]
        for d in range(2):
            keys += [("ga", t, d), ("gb", t, d, 0), ("gb", t, d, 1)]
    return {key: at for at, key in enumerate(keys)}


KEYS = sem_keys()


def kernel(
    a_hbm, h_hbm, w_hbm, accept_hbm, shrink_hbm,
    wg, g_out, stat_out,
    a_buf, a_hi, a_lo, h_f32, h_hi, h_lo,
    ah, ra, rb, rc, rd,
    s1, s2, t1, t_sum, t2, t3, t_all, hh_buf,
    w_own, flags_raw, powers_raw, flags, factors, base, updated,
    acc, wtw, core_in, ga, gb, a1, a2, a3,
    send_sem, recv_sem, a_sem, in_sem,
):
    rho, col = lax.axis_index("row"), lax.axis_index("col")
    y, z = lax.div(col, 4), lax.rem(col, 4)
    x, core = lax.div(rho, 2), lax.rem(rho, 2)
    along, across = (y, z), (z, y)

    def at_y(d):
        return (rho, lax.rem(y + d, 4) * 4 + z)

    def at_z(d):
        return (rho, y * 4 + lax.rem(z + d, 4))

    def at_row(d):
        return (lax.rem(rho + d, 8), col)

    def at_x(d):
        return (lax.rem(x + d, 4) * 2 + core, col)

    partner = (x * 2 + 1 - core, col)
    step_p, step_q = (at_y, at_z), (at_z, at_y)
    way = (1, 3)

    def row(f, dp, dq):
        return pl.multiple_of(
            f * FLOW + GROUP * lax.rem(along[f] + dp, 4) + PIECE * lax.rem(across[f] + dq, 4), PIECE
        )

    def piece(ref, f, dp, dq, start=0, size=PIECE):
        return ref.at[pl.ds(pl.multiple_of(row(f, dp, dq) + start, 64), size), :]

    sent = []

    def make(key, src, dst, to):
        return pltpu.make_async_remote_copy(
            src_ref=src, dst_ref=dst, send_sem=send_sem.at[KEYS[key]], recv_sem=recv_sem.at[KEYS[key]],
            device_id=to, device_id_type=MESH,
        )

    def send(key, src, dst, to):
        make(key, src(), dst(), to()).start()
        sent.append((key, src, dst, to))

    def arrived(key, dst, to):
        make(key, dst, dst, to).wait_recv()

    def chunk_row(j):
        f, t = lax.rem(j, 2), lax.div(j, 2)
        dp = 2 - t + 3 * lax.div(t, 2) - 2 * lax.div(t, 3)
        return pl.multiple_of(f * FLOW + GROUP * lax.rem(y + f * (z - y) + dp, 4), GROUP)

    def a_copy(j):
        slot = lax.rem(j, 2)
        return pltpu.make_async_copy(a_hbm.at[pl.ds(chunk_row(j), GROUP), :], a_buf.at[slot], a_sem.at[slot])

    h_copy = pltpu.make_async_copy(h_hbm, h_f32, in_sem.at[0])
    h_copy.start()
    a_copy(jnp.int32(0)).start()
    small = [
        pltpu.make_async_copy(accept_hbm, flags_raw, in_sem.at[1]),
        pltpu.make_async_copy(shrink_hbm, powers_raw, in_sem.at[2]),
        pltpu.make_async_copy(piece(w_hbm, 0, 0, 0), w_own.at[pl.ds(0, PIECE), :], in_sem.at[3]),
        pltpu.make_async_copy(piece(w_hbm, 1, 0, 0), w_own.at[pl.ds(PIECE, PIECE), :], in_sem.at[4]),
    ]
    barrier = pltpu.get_barrier_semaphore()
    peers = [at_row(d) for d in range(1, 8)] + [at_y(d) for d in range(1, 4)] + [at_z(d) for d in range(1, 4)]
    for peer in peers:
        pl.semaphore_signal(barrier, inc=1, device_id=peer, device_id_type=MESH)

    h_copy.wait()
    hi, lo = halves(h_f32[...])
    h_hi[...] = hi
    h_lo[...] = lo
    a_copy(jnp.int32(1)).start()
    for copy in small:
        copy.start()
    part = jnp.concatenate(halves(h_f32[pl.ds(pl.multiple_of(rho * 32, 32), 32), :]), axis=0)
    two = mmt(part, h_hi[...]) + mmt(part, h_lo[...])
    s1[z] = two[:32] + two[32:]

    def greeted():
        pl.semaphore_wait(barrier, len(peers))
        for d in range(1, 4):
            send(("s1", d), lambda: s1.at[z], lambda: s1.at[z], lambda d=d: at_z(d))

    def gram_y():
        for d in range(1, 4):
            arrived(("s1", d), s1.at[lax.rem(z + 4 - d, 4)], at_z(d))
        s2[y] = s1[0] + s1[1] + s1[2] + s1[3]
        for d in range(1, 4):
            send(("s2", d), lambda: s2.at[y], lambda: s2.at[y], lambda d=d: at_y(d))

    def gram_row():
        for d in range(1, 4):
            arrived(("s2", d), s2.at[lax.rem(y + 4 - d, 4)], at_y(d))
        hh_buf[rho] = s2[0] + s2[1] + s2[2] + s2[3]
        for d in range(1, 8):
            send(("s4", d), lambda: hh_buf.at[rho], lambda: hh_buf.at[rho], lambda d=d: at_row(d))

    def opposite(f):
        for d in range(2):
            for i, r in enumerate(RELAY[d]):
                send(("ra", f, d, r), lambda r=r: piece(ah, f, 2, r), lambda d=d, i=i: ra.at[f, d, i],
                     lambda d=d: step_p[f](way[d]))

    def near(f, d, r):
        send(("rb", f, d, r), lambda: piece(ah, f, way[d], r), lambda: rb.at[f, d, r], lambda: step_p[f](way[d]))

    def relayed(f, d, r):
        i = RELAY[d].index(r)
        arrived(("ra", f, d, r), ra.at[f, d, i], step_p[f](way[d]))
        at = pl.ds(row(f, way[d], r), PIECE)
        ah[at, :] += ra[f, d, i]
        near(f, d, r)

    hooks = {
        0: [greeted, lambda: opposite(0)],
        1: [lambda: opposite(1)],
        2: [lambda: near(0, 0, 3)],
        3: [lambda: near(1, 0, 3)],
        4: [lambda: near(0, 1, 2), lambda: relayed(0, 0, 2), gram_y],
        5: [lambda: near(1, 1, 2), lambda: relayed(1, 0, 2), lambda: near(0, 1, 1), lambda: relayed(0, 0, 1)],
        6: [lambda: near(1, 1, 1), lambda: relayed(1, 0, 1), lambda: relayed(0, 1, 3)],
        7: [lambda: relayed(1, 1, 3)],
    }

    @pl.loop(0, 8)
    def _(j):
        slot = lax.rem(j, 2)
        at = pl.ds(chunk_row(j), GROUP)
        a_copy(j).wait()
        hi, lo = halves(a_buf[slot])
        a_hi[at, :] = hi
        a_lo[at, :] = lo

        @pl.when(j < 6)
        def _():
            a_copy(j + 2).start()

        ah[at, :] = mmt(a_hi[at, :], h_hi[...]) + mmt(a_hi[at, :], h_lo[...]) + mmt(a_lo[at, :], h_hi[...])
        for when, steps in hooks.items():

            @pl.when(j == when)
            def _(steps=steps):
                for step in steps:
                    step()

    def own_sum(f, r):
        for d in range(2):
            arrived(("rb", f, d, r), rb.at[f, d, r], step_p[f](way[d]))
        at = pl.ds(row(f, 0, r), PIECE)
        ah[at, :] += rb[f, 0, r] + rb[f, 1, r]

    def half(f, r, start):
        return lambda: piece(ah, f, 0, r, start, 64)

    def last(f, d, part):
        start = 64 * d if part == 0 else 64 * (1 - d)
        send(("rd", f, d, part), half(f, way[d], start), lambda: rd.at[f, d, pl.ds(start, 64), :],
             lambda: step_q[f](way[d]))

    for f in range(2):
        own_sum(f, 2)
        for d in range(2):
            send(("rc", f, d), half(f, 2, 64 * d), lambda f=f, d=d: rc.at[f, d], lambda f=f, d=d: step_q[f](way[d]))

    for f in range(2):
        near(f, 0, 0)
        relayed(f, 1, 0)
    gram_row()
    for copy in small:
        copy.wait()
    acc[...] = jnp.zeros_like(acc)
    def down(line):
        return jnp.broadcast_to(line, (PIECE, PIECE)).T

    for f in range(2):
        lanes = pl.ds(row(f, 0, 0), PIECE)
        for t in range(2):
            at = slice(f * PIECE, (f + 1) * PIECE)
            flags[t, at, :] = down(flags_raw[t : t + 1, lanes].astype(F32))
            power = powers_raw[t : t + 1, lanes]
            scale = jnp.where(power == 0, 1.0, jnp.where(power == 1, 0.5, jnp.where(power == 2, 0.25, 0.125)))
            factors[t, at, :] = down(scale.astype(F32))

    for d, r in ((0, 1), (1, 3)):
        for f in range(2):
            own_sum(f, r)
            last(f, d, 1)
    for f in range(2):
        for d in range(2):
            arrived(("rc", f, d), rc.at[f, d], step_q[f](way[d]))
            at = pl.ds(pl.multiple_of(row(f, 0, way[d]) + 64 * d, 64), 64)
            ah[at, :] += rc[f, d]
            last(f, d, 0)
    for d in range(1, 8):
        arrived(("s4", d), hh_buf.at[lax.rem(rho + 8 - d, 8)], at_row(d))
    hh = hh_buf[...].reshape(RANK, RANK)
    base[...] = exact(w_own[...], hh)

    for f in range(2):
        own_sum(f, 0)
    own = [pl.ds(row(f, 0, 0), PIECE) for f in range(2)]

    both = (RANK, RANK)
    eye = lax.broadcasted_iota(jnp.int32, both, 0) == lax.broadcasted_iota(jnp.int32, both, 1)
    step_size = float(RANK) / jnp.sum(jnp.where(eye, hh, 0.0), keepdims=True)

    def twice(v):
        return jnp.concatenate([v, v], axis=1)

    def trials(f):
        for d in range(2):
            for part in range(2):
                start = 64 * d if part == 0 else 64 * (1 - d)
                arrived(("rd", f, d, part), rd.at[f, d, pl.ds(start, 64), :], step_q[f](way[d]))
        at = slice(f * PIECE, (f + 1) * PIECE)
        current = w_own[at, :]
        gradient = base[at, :] - (ah[own[f], :] + rd[f, 0] + rd[f, 1])
        sums = []
        for t in range(2):
            change = jnp.maximum(current - twice(factors[t, at, :]) * step_size * gradient, 0.0) - current
            sums.append(jnp.sum(gradient * change, keepdims=True))
            current = current + twice(flags[t, at, :]) * change
            if t == 0:
                turned = exact(change, hh)
                sums.append(jnp.sum(change * turned, keepdims=True))
                gradient = gradient + twice(flags[t, at, :]) * turned
        wg[own[f], :] = current
        for d in range(2):
            send(("g1", f, d), lambda: piece(wg, f, 0, 0), lambda: piece(wg, f, 0, 0),
                 lambda d=d: step_q[f](way[d]))
        updated[at, :] = current
        return sums, change

    def spread(f, r):
        for d in range(2):
            send(("g2", f, d, r), lambda: piece(wg, f, 0, r), lambda: piece(wg, f, 0, r),
                 lambda d=d: step_p[f](way[d]))

    made = [trials(0), trials(1)]
    ends = jnp.concatenate([change for _, change in made], axis=0)
    sums = [first_ + second_ for first_, second_ in zip(made[0][0], made[1][0])]
    sums.append(jnp.sum(ends * exact(ends, hh), keepdims=True))
    place = lax.broadcasted_iota(jnp.int32, (8, 128), 0) * 2 + lax.broadcasted_iota(jnp.int32, (8, 128), 1)
    stats = jnp.zeros((8, 128), F32)
    for at, value in enumerate(sums):
        stats = jnp.where(place == at, value, stats)
    a1[rho] = stats
    for d in range(1, 8):
        send(("a1", d), lambda: a1.at[rho], lambda: a1.at[rho], lambda d=d: at_row(d))

    current = updated[...]
    c_hi, c_lo = halves(current)
    d_hi, d_lo = halves(current.T)
    wtw[...] = mm(d_hi, c_hi) + mm(d_lo, c_hi) + mm(d_hi, c_lo)

    def rows_of(ref, k, size):
        return ref.at[pl.ds(pl.multiple_of(size * k, size), size), :]

    for d in range(1, 8):
        send(("t1", d), lambda d=d: rows_of(wtw, lax.rem(rho + d, 8), 32), lambda: t1.at[rho], lambda d=d: at_row(d))

    def factor_z():
        t1[rho] = wtw[pl.ds(pl.multiple_of(32 * rho, 32), 32), :]
        for d in range(1, 8):
            arrived(("t1", d), t1.at[lax.rem(rho + 8 - d, 8)], at_row(d))
        rows = t1[0]
        for k in range(1, 8):
            rows = rows + t1[k]
        t_sum[...] = rows
        for d in range(1, 4):
            send(("t2", d), lambda d=d: rows_of(t_sum, lax.rem(z + d, 4), 8), lambda: t2.at[z], lambda d=d: at_z(d))

    def factor_y():
        t2[z] = t_sum[pl.ds(pl.multiple_of(8 * z, 8), 8), :]
        for d in range(1, 4):
            arrived(("t2", d), t2.at[lax.rem(z + 4 - d, 4)], at_z(d))
        t3[y] = t2[0] + t2[1] + t2[2] + t2[3]
        for d in range(1, 4):
            send(("t3", d), lambda: t3.at[y], lambda: t3.at[y], lambda d=d: at_y(d))

    def factor_all():
        for d in range(1, 4):
            arrived(("t3", d), t3.at[lax.rem(y + 4 - d, 4)], at_y(d))
        t_all[pl.ds(pl.multiple_of(8 * z, 8), 8), :] = t3[0] + t3[1] + t3[2] + t3[3]
        for d in range(1, 4):
            send(("t4", d), lambda: rows_of(t_all, z, 8), lambda: rows_of(t_all, z, 8), lambda d=d: at_z(d))

    def stats_y():
        for d in range(1, 8):
            arrived(("a1", d), a1.at[lax.rem(rho + 8 - d, 8)], at_row(d))
        a2[y] = sum(a1[k] for k in range(1, 8)) + a1[0]
        for d in range(1, 4):
            send(("a2", d), lambda: a2.at[y], lambda: a2.at[y], lambda d=d: at_y(d))

    def stats_z():
        for d in range(1, 4):
            arrived(("a2", d), a2.at[lax.rem(y + 4 - d, 4)], at_y(d))
        a3[z] = a2[0] + a2[1] + a2[2] + a2[3]
        for d in range(1, 4):
            send(("a3", d), lambda: a3.at[z], lambda: a3.at[z], lambda d=d: at_z(d))

    def beside(f):
        for d in range(2):
            r = 4 - way[d]
            arrived(("g1", f, d), piece(wg, f, 0, r), step_q[f](way[d]))
            send(("g1h", f, d), lambda r=r, d=d: piece(wg, f, 0, r, 64 * d, 64),
                 lambda r=r, d=d: piece(wg, f, 0, r, 64 * d, 64), lambda d=d: step_q[f](way[d]))

    def across_ring(f):
        for d in range(2):
            arrived(("g1h", f, d), piece(wg, f, 0, 2, 64 * d, 64), step_q[f](way[d]))
        spread(f, 2)

    def come(f, r):
        for d in range(2):
            arrived(("g2", f, d, r), piece(wg, f, 4 - way[d], r), step_p[f](way[d]))

    def onward(f, r):
        for d in range(2):
            dp = 4 - way[d]
            send(("g2h", f, d, r), lambda dp=dp, d=d: piece(wg, f, dp, r, 64 * d, 64),
                 lambda dp=dp, d=d: piece(wg, f, dp, r, 64 * d, 64), lambda d=d: step_p[f](way[d]))

    def far(f, r):
        for d in range(2):
            arrived(("g2h", f, d, r), piece(wg, f, 2, r, 64 * d, 64), step_p[f](way[d]))

    def pair(step, *given):
        return lambda: [step(f, *given) for f in range(2)]

    before = {
        0: [pair(spread, 0), pair(beside), pair(spread, 1), pair(spread, 3)],
        1: [pair(come, 0)],
        2: [pair(across_ring), stats_y, factor_z, pair(onward, 0)],
        3: [pair(come, 1), pair(onward, 1)],
        4: [pair(come, 3), pair(onward, 3)],
        5: [pair(come, 2), pair(onward, 2), stats_z, factor_y],
        6: [pair(far, 0), pair(far, 1)],
        7: [pair(far, 3), pair(far, 2)],
    }
    order = (((0, 0), (0, 1)), ((1, 0), (3, 0)), ((0, 3), (0, 2)), ((1, 1), (3, 1)),
             ((1, 3), (3, 3)), ((1, 2), (3, 2)), ((2, 0), (2, 1)), ((2, 3), (2, 2)))
    codes = tuple(
        jnp.int32(sum(cell[n][i] * 4**u for u, cell in enumerate(order))) for n in range(2) for i in range(2)
    )

    def factor_halves(at):
        return halves(jnp.concatenate([wg[rows, :] for rows in at], axis=0).T)

    def block(t, k, mine, start=0, size=32):
        at = 64 * lax.rem(x + k, 4) + 32 * (core if mine else 1 - core) + start
        return (t, pl.ds(pl.multiple_of(at, 16), size), slice(None))

    def to_partner(t):
        for k in (2, 1, 3, 0):
            send(("core", t, k), lambda k=k: acc.at[block(t, k, False)], lambda k=k: core_in.at[t, k], lambda: partner)

    def unit(u, codes):
        for when, steps in before.items():

            @pl.when(u == when)
            def _(steps=steps):
                for step in steps:
                    step()

        at = []
        for n in range(2):
            dp, r = lax.rem(codes[2 * n], 4), lax.rem(codes[2 * n + 1], 4)
            at += [pl.ds(row(f, dp, r), PIECE) for f in range(2)]
        left_hi, left_lo = factor_halves(at)
        for t in range(TILES):
            cols = slice(t * WIDTH, (t + 1) * WIDTH)
            m_hi = jnp.concatenate([a_hi[rows, cols] for rows in at], axis=0)
            m_lo = jnp.concatenate([a_lo[rows, cols] for rows in at], axis=0)
            acc[t] = acc[t] + mm(left_hi, m_hi) + mm(left_lo, m_hi) + mm(left_hi, m_lo)
        return tuple(lax.div(code, 4) for code in codes)

    lax.fori_loop(0, 8, unit, codes)

    def joined(t, k):
        arrived(("core", t, k), core_in.at[t, k], partner)
        acc[block(t, k, True)] += core_in[t, k]

    def first(t):
        joined(t, 2)
        for d in range(2):
            send(("ga", t, d), lambda d=d: acc.at[block(t, 2, True, 16 * d, 16)], lambda d=d: ga.at[t, d],
                 lambda d=d: at_x(way[d]))

    def beyond(t):
        for d in range(2):
            joined(t, way[d])
            onto(t, d, 1)
        joined(t, 0)

    def onto(t, d, part):
        start = 16 * d if part == 0 else 16 * (1 - d)
        send(("gb", t, d, part), lambda: acc.at[block(t, way[d], True, start, 16)],
             lambda: gb.at[t, d, pl.ds(start, 16), :], lambda: at_x(way[d]))

    def second(t):
        for d in range(2):
            arrived(("ga", t, d), ga.at[t, d], at_x(way[d]))
            acc[block(t, way[d], True, 16 * d, 16)] += ga[t, d]
            onto(t, d, 0)

    def third(t):
        for d in range(2):
            for part in range(2):
                start = 16 * d if part == 0 else 16 * (1 - d)
                arrived(("gb", t, d, part), gb.at[t, d, pl.ds(start, 16), :], at_x(way[d]))
        g_out[:, t * WIDTH : (t + 1) * WIDTH] -= acc[block(t, 0, True)] + gb[t, 0] + gb[t, 1]

    def leave(items):
        for key, src, dst, to in items:
            make(key, src(), dst(), to()).wait_send()

    before_tail = list(sent)
    for t in range(TILES):
        to_partner(t)
    for t in range(TILES):
        first(t)
    for t in range(TILES):
        beyond(t)
    factor_all()
    for t in range(TILES):
        second(t)
    leave(before_tail)
    for d in range(1, 4):
        arrived(("t4", d), rows_of(t_all, lax.rem(z + 4 - d, 4), 8), at_z(d))
    t_hi, t_lo = halves(t_all[...])
    for t in range(TILES):
        cols = slice(t * WIDTH, (t + 1) * WIDTH)
        g_out[:, cols] = mm(t_hi, h_hi[:, cols]) + mm(t_hi, h_lo[:, cols]) + mm(t_lo, h_hi[:, cols])
    for d in range(1, 4):
        arrived(("a3", d), a3.at[lax.rem(z + 4 - d, 4)], at_z(d))
    stat_out[...] = (a3[0] + a3[1] + a3[2] + a3[3])[:2, :2]
    for t in range(TILES):
        third(t)
    leave(sent[len(before_tail) :])


def hand_over(w_in, g_in, stat_in, w_out, g_out, stat_out, out_sem):
    copies = [
        pltpu.make_async_copy(source, target, out_sem.at[n])
        for n, (source, target) in enumerate(((w_in, w_out), (g_in, g_out), (stat_in, stat_out)))
    ]
    for copy in copies:
        copy.start()
    for copy in copies:
        copy.wait()


def per_device(a_matrix, h_factor, w_factor, accept, shrink):
    vmem = pltpu.VMEM
    anywhere = pl.BlockSpec(memory_space=pl.ANY)
    inside = pl.BlockSpec(memory_space=vmem)
    results = pl.pallas_call(
        kernel,
        out_shape=(
            vmem((ROWS, RANK), F32),
            vmem((RANK // 8, COLS), F32),
            vmem((2, 2), F32),
        ),
        in_specs=[anywhere] * 5,
        out_specs=(inside, inside, inside),
        scratch_shapes=[
            vmem((2, GROUP, COLS), F32),
            vmem((ROWS, COLS), BF16),
            vmem((ROWS, COLS), BF16),
            vmem((RANK, COLS), F32),
            vmem((RANK, COLS), BF16),
            vmem((RANK, COLS), BF16),
            vmem((ROWS, RANK), F32),
            vmem((2, 2, 2, PIECE, RANK), F32),
            vmem((2, 2, 4, PIECE, RANK), F32),
            vmem((2, 2, 64, RANK), F32),
            vmem((2, 2, PIECE, RANK), F32),
            vmem((4, 32, RANK), F32),
            vmem((4, 32, RANK), F32),
            vmem((8, 32, RANK), F32),
            vmem((32, RANK), F32),
            vmem((4, 8, RANK), F32),
            vmem((4, 8, RANK), F32),
            vmem((32, RANK), F32),
            vmem((8, 32, RANK), F32),
            vmem((RANK, RANK), F32),
            vmem((2, ROWS), jnp.int32),
            vmem((2, ROWS), jnp.int32),
            vmem((2, RANK, PIECE), F32),
            vmem((2, RANK, PIECE), F32),
            vmem((RANK, RANK), F32),
            vmem((RANK, RANK), F32),
            vmem((TILES, RANK, WIDTH), F32),
            vmem((RANK, RANK), F32),
            vmem((TILES, 4, 32, WIDTH), F32),
            vmem((TILES, 2, 16, WIDTH), F32),
            vmem((TILES, 2, 32, WIDTH), F32),
            vmem((8, 8, 128), F32),
            vmem((4, 8, 128), F32),
            vmem((4, 8, 128), F32),
            pltpu.SemaphoreType.DMA((len(KEYS),)),
            pltpu.SemaphoreType.DMA((len(KEYS),)),
            pltpu.SemaphoreType.DMA((2,)),
            pltpu.SemaphoreType.DMA((5,)),
        ],
        compiler_params=pltpu.CompilerParams(
            collective_id=0, has_side_effects=True, vmem_limit_bytes=58 * 1024 * 1024
        ),
    )(a_matrix, h_factor, w_factor, accept.T, shrink.T)
    held = [pltpu.with_memory_space_constraint(result, vmem) for result in results]
    return pl.pallas_call(
        hand_over,
        out_shape=(
            jax.ShapeDtypeStruct((ROWS, RANK), F32),
            jax.ShapeDtypeStruct((RANK // 8, COLS), F32),
            jax.ShapeDtypeStruct((2, 2), F32),
        ),
        in_specs=[inside, inside, inside],
        out_specs=(anywhere, anywhere, anywhere),
        scratch_shapes=[pltpu.SemaphoreType.DMA((3,))],
        compiler_params=pltpu.CompilerParams(vmem_limit_bytes=8 * 1024 * 1024),
    )(*held)

def solution(mesh):
    in_specs = (P("row", "col"), P(None, "col"), P("row", None), P("row", None), P("row", None))
    out_specs = (P("row", None), P("row", "col"), P())
    return jax.shard_map(per_device, mesh=mesh, in_specs=in_specs, out_specs=out_specs, check_vma=False)
```

```python
import functools

import jax
import jax.numpy as jnp
from jax import lax
from jax.experimental import pallas as pl
from jax.experimental.pallas import tpu as pltpu
from jax.sharding import PartitionSpec as P

F32, BF16 = jnp.float32, jnp.bfloat16
MESH = pl.DeviceIdType.MESH
RANK, ROWS, COLS = 256, 4096, 1536
PIECE, GROUP, FLOW = 128, 512, 2048
TILES = 1
WIDTH = COLS // TILES
RELAY = (((2, 1), (3, 0)))


def halves(x):
    hi = x.astype(BF16)
    return hi, (x - hi.astype(F32)).astype(BF16)


def mm(a, b):
    return lax.dot_general(a, b, (((1,), (0,)), ((), ())), preferred_element_type=F32)


def mmt(a, b):
    return lax.dot_general(a, b, (((1,), (1,)), ((), ())), preferred_element_type=F32)


def exact(a, b):
    return jnp.dot(a, b, precision=lax.Precision.HIGHEST, preferred_element_type=F32)


def sem_keys():
    keys = []
    for f in range(2):
        for d in range(2):
            keys += [("ra", f, d, r) for r in RELAY[d]]
            keys += [("rb", f, d, r) for r in range(4)]
            keys += [("rc", f, d), ("rd", f, d, 0), ("rd", f, d, 1)]
            keys += [("g1", f, d), ("g1h", f, d)]
            keys += [("g2", f, d, r) for r in range(4)]
            keys += [("g2h", f, d, r) for r in range(4)]
    for name, count in (("s1", 4), ("s2", 4), ("s4", 8), ("t1", 8), ("t2", 4), ("t3", 4), ("t4", 4), ("a1", 8), ("a2", 4), ("a3", 4)):
        keys += [(name, d) for d in range(1, count)]
    for t in range(TILES):
        keys += [("core", t, k) for k in range(4)]
        for d in range(2):
            keys += [("ga", t, d), ("gb", t, d, 0), ("gb", t, d, 1)]
    return {key: at for at, key in enumerate(keys)}


KEYS = sem_keys()


def kernel(
    a_hbm, h_hbm, w_hbm, accept_hbm, shrink_hbm,
    wg, g_out, stat_out,
    a_buf, a_hi, a_lo, h_f32, h_hi, h_lo,
    ah, ra, rb, rc, rd,
    s1, s2, t1, t_sum, t2, t3, t_all, hh_buf,
    w_own, flags_raw, powers_raw, flags, factors, base, updated,
    acc, wtw, core_in, ga, gb, a1, a2, a3,
    send_sem, recv_sem, a_sem, in_sem,
):
    rho, col = lax.axis_index("row"), lax.axis_index("col")
    y, z = lax.div(col, 4), lax.rem(col, 4)
    x, core = lax.div(rho, 2), lax.rem(rho, 2)
    along, across = (y, z), (z, y)

    def at_y(d):
        return (rho, lax.rem(y + d, 4) * 4 + z)

    def at_z(d):
        return (rho, y * 4 + lax.rem(z + d, 4))

    def at_row(d):
        return (lax.rem(rho + d, 8), col)

    def at_x(d):
        return (lax.rem(x + d, 4) * 2 + core, col)

    partner = (x * 2 + 1 - core, col)
    step_p, step_q = (at_y, at_z), (at_z, at_y)
    way = (1, 3)

    def row(f, dp, dq):
        return pl.multiple_of(
            f * FLOW + GROUP * lax.rem(along[f] + dp, 4) + PIECE * lax.rem(across[f] + dq, 4), PIECE
        )

    def piece(ref, f, dp, dq, start=0, size=PIECE):
        return ref.at[pl.ds(pl.multiple_of(row(f, dp, dq) + start, 64), size), :]

    sent = []

    def make(key, src, dst, to):
        return pltpu.make_async_remote_copy(
            src_ref=src, dst_ref=dst, send_sem=send_sem.at[KEYS[key]], recv_sem=recv_sem.at[KEYS[key]],
            device_id=to, device_id_type=MESH,
        )

    def send(key, src, dst, to):
        make(key, src(), dst(), to()).start()
        sent.append((key, src, dst, to))

    def arrived(key, dst, to):
        make(key, dst, dst, to).wait_recv()

    def chunk_row(j):
        f, t = lax.rem(j, 2), lax.div(j, 2)
        dp = 2 - t + 3 * lax.div(t, 2) - 2 * lax.div(t, 3)
        return pl.multiple_of(f * FLOW + GROUP * lax.rem(y + f * (z - y) + dp, 4), GROUP)

    def a_copy(j):
        slot = lax.rem(j, 2)
        return pltpu.make_async_copy(a_hbm.at[pl.ds(chunk_row(j), GROUP), :], a_buf.at[slot], a_sem.at[slot])

    h_copy = pltpu.make_async_copy(h_hbm, h_f32, in_sem.at[0])
    h_copy.start()
    a_copy(jnp.int32(0)).start()
    small = [
        pltpu.make_async_copy(accept_hbm, flags_raw, in_sem.at[1]),
        pltpu.make_async_copy(shrink_hbm, powers_raw, in_sem.at[2]),
        pltpu.make_async_copy(piece(w_hbm, 0, 0, 0), w_own.at[pl.ds(0, PIECE), :], in_sem.at[3]),
        pltpu.make_async_copy(piece(w_hbm, 1, 0, 0), w_own.at[pl.ds(PIECE, PIECE), :], in_sem.at[4]),
    ]
    barrier = pltpu.get_barrier_semaphore()
    peers = [at_row(d) for d in range(1, 8)] + [at_y(d) for d in range(1, 4)] + [at_z(d) for d in range(1, 4)]
    for peer in peers:
        pl.semaphore_signal(barrier, inc=1, device_id=peer, device_id_type=MESH)

    h_copy.wait()
    hi, lo = halves(h_f32[...])
    h_hi[...] = hi
    h_lo[...] = lo
    a_copy(jnp.int32(1)).start()
    for copy in small:
        copy.start()
    part = jnp.concatenate(halves(h_f32[pl.ds(pl.multiple_of(rho * 32, 32), 32), :]), axis=0)
    two = mmt(part, h_hi[...]) + mmt(part, h_lo[...])
    s1[z] = two[:32] + two[32:]

    def greeted():
        pl.semaphore_wait(barrier, len(peers))
        for d in range(1, 4):
            send(("s1", d), lambda: s1.at[z], lambda: s1.at[z], lambda d=d: at_z(d))

    def gram_y():
        for d in range(1, 4):
            arrived(("s1", d), s1.at[lax.rem(z + 4 - d, 4)], at_z(d))
        s2[y] = s1[0] + s1[1] + s1[2] + s1[3]
        for d in range(1, 4):
            send(("s2", d), lambda: s2.at[y], lambda: s2.at[y], lambda d=d: at_y(d))

    def gram_row():
        for d in range(1, 4):
            arrived(("s2", d), s2.at[lax.rem(y + 4 - d, 4)], at_y(d))
        hh_buf[rho] = s2[0] + s2[1] + s2[2] + s2[3]
        for d in range(1, 8):
            send(("s4", d), lambda: hh_buf.at[rho], lambda: hh_buf.at[rho], lambda d=d: at_row(d))

    def opposite(f):
        for d in range(2):
            for i, r in enumerate(RELAY[d]):
                send(("ra", f, d, r), lambda r=r: piece(ah, f, 2, r), lambda d=d, i=i: ra.at[f, d, i],
                     lambda d=d: step_p[f](way[d]))

    def near(f, d, r):
        send(("rb", f, d, r), lambda: piece(ah, f, way[d], r), lambda: rb.at[f, d, r], lambda: step_p[f](way[d]))

    def relayed(f, d, r):
        i = RELAY[d].index(r)
        arrived(("ra", f, d, r), ra.at[f, d, i], step_p[f](way[d]))
        at = pl.ds(row(f, way[d], r), PIECE)
        ah[at, :] += ra[f, d, i]
        near(f, d, r)

    hooks = {
        0: [greeted, lambda: opposite(0)],
        1: [lambda: opposite(1)],
        2: [lambda: near(0, 0, 3)],
        3: [lambda: near(1, 0, 3)],
        4: [lambda: near(0, 1, 2), lambda: relayed(0, 0, 2), gram_y],
        5: [lambda: near(1, 1, 2), lambda: relayed(1, 0, 2), lambda: near(0, 1, 1), lambda: relayed(0, 0, 1)],
        6: [lambda: near(1, 1, 1), lambda: relayed(1, 0, 1), lambda: relayed(0, 1, 3)],
        7: [lambda: relayed(1, 1, 3)],
    }

    @pl.loop(0, 8)
    def _(j):
        slot = lax.rem(j, 2)
        at = pl.ds(chunk_row(j), GROUP)
        a_copy(j).wait()
        hi, lo = halves(a_buf[slot])
        a_hi[at, :] = hi
        a_lo[at, :] = lo

        @pl.when(j < 6)
        def _():
            a_copy(j + 2).start()

        ah[at, :] = mmt(a_hi[at, :], h_hi[...]) + mmt(a_hi[at, :], h_lo[...]) + mmt(a_lo[at, :], h_hi[...])
        for when, steps in hooks.items():

            @pl.when(j == when)
            def _(steps=steps):
                for step in steps:
                    step()

    def own_sum(f, r):
        for d in range(2):
            arrived(("rb", f, d, r), rb.at[f, d, r], step_p[f](way[d]))
        at = pl.ds(row(f, 0, r), PIECE)
        ah[at, :] += rb[f, 0, r] + rb[f, 1, r]

    def half(f, r, start):
        return lambda: piece(ah, f, 0, r, start, 64)

    def last(f, d, part):
        start = 64 * d if part == 0 else 64 * (1 - d)
        send(("rd", f, d, part), half(f, way[d], start), lambda: rd.at[f, d, pl.ds(start, 64), :],
             lambda: step_q[f](way[d]))

    for f in range(2):
        own_sum(f, 2)
        for d in range(2):
            send(("rc", f, d), half(f, 2, 64 * d), lambda f=f, d=d: rc.at[f, d], lambda f=f, d=d: step_q[f](way[d]))

    for f in range(2):
        near(f, 0, 0)
        relayed(f, 1, 0)
    gram_row()
    for copy in small:
        copy.wait()
    acc[...] = jnp.zeros_like(acc)
    def down(line):
        return jnp.broadcast_to(line, (PIECE, PIECE)).T

    for f in range(2):
        lanes = pl.ds(row(f, 0, 0), PIECE)
        for t in range(2):
            at = slice(f * PIECE, (f + 1) * PIECE)
            flags[t, at, :] = down(flags_raw[t : t + 1, lanes].astype(F32))
            power = powers_raw[t : t + 1, lanes]
            scale = jnp.where(power == 0, 1.0, jnp.where(power == 1, 0.5, jnp.where(power == 2, 0.25, 0.125)))
            factors[t, at, :] = down(scale.astype(F32))

    for d, r in ((0, 1), (1, 3)):
        for f in range(2):
            own_sum(f, r)
            last(f, d, 1)
    for f in range(2):
        for d in range(2):
            arrived(("rc", f, d), rc.at[f, d], step_q[f](way[d]))
            at = pl.ds(pl.multiple_of(row(f, 0, way[d]) + 64 * d, 64), 64)
            ah[at, :] += rc[f, d]
            last(f, d, 0)
    for d in range(1, 8):
        arrived(("s4", d), hh_buf.at[lax.rem(rho + 8 - d, 8)], at_row(d))
    hh = hh_buf[...].reshape(RANK, RANK)
    base[...] = exact(w_own[...], hh)

    for f in range(2):
        own_sum(f, 0)
    own = [pl.ds(row(f, 0, 0), PIECE) for f in range(2)]

    both = (RANK, RANK)
    eye = lax.broadcasted_iota(jnp.int32, both, 0) == lax.broadcasted_iota(jnp.int32, both, 1)
    step_size = float(RANK) / jnp.sum(jnp.where(eye, hh, 0.0), keepdims=True)

    def twice(v):
        return jnp.concatenate([v, v], axis=1)

    def trials(f):
        for d in range(2):
            for part in range(2):
                start = 64 * d if part == 0 else 64 * (1 - d)
                arrived(("rd", f, d, part), rd.at[f, d, pl.ds(start, 64), :], step_q[f](way[d]))
        at = slice(f * PIECE, (f + 1) * PIECE)
        current = w_own[at, :]
        gradient = base[at, :] - (ah[own[f], :] + rd[f, 0] + rd[f, 1])
        sums = []
        for t in range(2):
            change = jnp.maximum(current - twice(factors[t, at, :]) * step_size * gradient, 0.0) - current
            sums.append(jnp.sum(gradient * change, keepdims=True))
            current = current + twice(flags[t, at, :]) * change
            if t == 0:
                turned = exact(change, hh)
                sums.append(jnp.sum(change * turned, keepdims=True))
                gradient = gradient + twice(flags[t, at, :]) * turned
        wg[own[f], :] = current
        for d in range(2):
            send(("g1", f, d), lambda: piece(wg, f, 0, 0), lambda: piece(wg, f, 0, 0),
                 lambda d=d: step_q[f](way[d]))
        updated[at, :] = current
        return sums, change

    def spread(f, r):
        for d in range(2):
            send(("g2", f, d, r), lambda: piece(wg, f, 0, r), lambda: piece(wg, f, 0, r),
                 lambda d=d: step_p[f](way[d]))

    made = [trials(0), trials(1)]
    ends = jnp.concatenate([change for _, change in made], axis=0)
    sums = [first_ + second_ for first_, second_ in zip(made[0][0], made[1][0])]
    sums.append(jnp.sum(ends * exact(ends, hh), keepdims=True))
    place = lax.broadcasted_iota(jnp.int32, (8, 128), 0) * 2 + lax.broadcasted_iota(jnp.int32, (8, 128), 1)
    stats = jnp.zeros((8, 128), F32)
    for at, value in enumerate(sums):
        stats = jnp.where(place == at, value, stats)
    a1[rho] = stats
    for d in range(1, 8):
        send(("a1", d), lambda: a1.at[rho], lambda: a1.at[rho], lambda d=d: at_row(d))

    current = updated[...]
    c_hi, c_lo = halves(current)
    d_hi, d_lo = halves(current.T)
    wtw[...] = mm(d_hi, c_hi) + mm(d_lo, c_hi) + mm(d_hi, c_lo)

    def rows_of(ref, k, size):
        return ref.at[pl.ds(pl.multiple_of(size * k, size), size), :]

    for d in range(1, 8):
        send(("t1", d), lambda d=d: rows_of(wtw, lax.rem(rho + d, 8), 32), lambda: t1.at[rho], lambda d=d: at_row(d))

    def factor_z():
        t1[rho] = wtw[pl.ds(pl.multiple_of(32 * rho, 32), 32), :]
        for d in range(1, 8):
            arrived(("t1", d), t1.at[lax.rem(rho + 8 - d, 8)], at_row(d))
        rows = t1[0]
        for k in range(1, 8):
            rows = rows + t1[k]
        t_sum[...] = rows
        for d in range(1, 4):
            send(("t2", d), lambda d=d: rows_of(t_sum, lax.rem(z + d, 4), 8), lambda: t2.at[z], lambda d=d: at_z(d))

    def factor_y():
        t2[z] = t_sum[pl.ds(pl.multiple_of(8 * z, 8), 8), :]
        for d in range(1, 4):
            arrived(("t2", d), t2.at[lax.rem(z + 4 - d, 4)], at_z(d))
        t3[y] = t2[0] + t2[1] + t2[2] + t2[3]
        for d in range(1, 4):
            send(("t3", d), lambda: t3.at[y], lambda: t3.at[y], lambda d=d: at_y(d))

    def factor_all():
        for d in range(1, 4):
            arrived(("t3", d), t3.at[lax.rem(y + 4 - d, 4)], at_y(d))
        t_all[pl.ds(pl.multiple_of(8 * z, 8), 8), :] = t3[0] + t3[1] + t3[2] + t3[3]
        for d in range(1, 4):
            send(("t4", d), lambda: rows_of(t_all, z, 8), lambda: rows_of(t_all, z, 8), lambda d=d: at_z(d))

    def stats_y():
        for d in range(1, 8):
            arrived(("a1", d), a1.at[lax.rem(rho + 8 - d, 8)], at_row(d))
        a2[y] = sum(a1[k] for k in range(1, 8)) + a1[0]
        for d in range(1, 4):
            send(("a2", d), lambda: a2.at[y], lambda: a2.at[y], lambda d=d: at_y(d))

    def stats_z():
        for d in range(1, 4):
            arrived(("a2", d), a2.at[lax.rem(y + 4 - d, 4)], at_y(d))
        a3[z] = a2[0] + a2[1] + a2[2] + a2[3]
        for d in range(1, 4):
            send(("a3", d), lambda: a3.at[z], lambda: a3.at[z], lambda d=d: at_z(d))

    def beside(f):
        for d in range(2):
            r = 4 - way[d]
            arrived(("g1", f, d), piece(wg, f, 0, r), step_q[f](way[d]))
            send(("g1h", f, d), lambda r=r, d=d: piece(wg, f, 0, r, 64 * d, 64),
                 lambda r=r, d=d: piece(wg, f, 0, r, 64 * d, 64), lambda d=d: step_q[f](way[d]))

    def across_ring(f):
        for d in range(2):
            arrived(("g1h", f, d), piece(wg, f, 0, 2, 64 * d, 64), step_q[f](way[d]))
        spread(f, 2)

    def come(f, r):
        for d in range(2):
            arrived(("g2", f, d, r), piece(wg, f, 4 - way[d], r), step_p[f](way[d]))

    def onward(f, r):
        for d in range(2):
            dp = 4 - way[d]
            send(("g2h", f, d, r), lambda dp=dp, d=d: piece(wg, f, dp, r, 64 * d, 64),
                 lambda dp=dp, d=d: piece(wg, f, dp, r, 64 * d, 64), lambda d=d: step_p[f](way[d]))

    def far(f, r):
        for d in range(2):
            arrived(("g2h", f, d, r), piece(wg, f, 2, r, 64 * d, 64), step_p[f](way[d]))

    def pair(step, *given):
        return lambda: [step(f, *given) for f in range(2)]

    before = {
        0: [pair(spread, 0), pair(beside), pair(spread, 1), pair(spread, 3)],
        1: [pair(come, 0)],
        2: [pair(across_ring), stats_y, factor_z, pair(onward, 0)],
        3: [pair(come, 1), pair(onward, 1)],
        4: [pair(come, 3), pair(onward, 3)],
        5: [pair(come, 2), pair(onward, 2), stats_z, factor_y],
        6: [pair(far, 0), pair(far, 1)],
        7: [pair(far, 3), pair(far, 2)],
    }
    order = (((0, 0), (0, 1)), ((1, 0), (3, 0)), ((0, 3), (0, 2)), ((1, 1), (3, 1)),
             ((1, 3), (3, 3)), ((1, 2), (3, 2)), ((2, 0), (2, 1)), ((2, 3), (2, 2)))
    codes = tuple(
        jnp.int32(sum(cell[n][i] * 4**u for u, cell in enumerate(order))) for n in range(2) for i in range(2)
    )

    def factor_halves(at):
        return halves(jnp.concatenate([wg[rows, :] for rows in at], axis=0).T)

    def block(t, k, mine, start=0, size=32):
        at = 64 * lax.rem(x + k, 4) + 32 * (core if mine else 1 - core) + start
        return (t, pl.ds(pl.multiple_of(at, 16), size), slice(None))

    def to_partner(t):
        for k in (2, 1, 3, 0):
            send(("core", t, k), lambda k=k: acc.at[block(t, k, False)], lambda k=k: core_in.at[t, k], lambda: partner)

    def unit(u, codes):
        for when, steps in before.items():

            @pl.when(u == when)
            def _(steps=steps):
                for step in steps:
                    step()

        at = []
        for n in range(2):
            dp, r = lax.rem(codes[2 * n], 4), lax.rem(codes[2 * n + 1], 4)
            at += [pl.ds(row(f, dp, r), PIECE) for f in range(2)]
        left_hi, left_lo = factor_halves(at)
        for t in range(TILES):
            cols = slice(t * WIDTH, (t + 1) * WIDTH)
            m_hi = jnp.concatenate([a_hi[rows, cols] for rows in at], axis=0)
            m_lo = jnp.concatenate([a_lo[rows, cols] for rows in at], axis=0)
            acc[t] = acc[t] + mm(left_hi, m_hi) + mm(left_lo, m_hi) + mm(left_hi, m_lo)
        return tuple(lax.div(code, 4) for code in codes)

    lax.fori_loop(0, 8, unit, codes)

    def joined(t, k):
        arrived(("core", t, k), core_in.at[t, k], partner)
        acc[block(t, k, True)] += core_in[t, k]

    def first(t):
        joined(t, 2)
        for d in range(2):
            send(("ga", t, d), lambda d=d: acc.at[block(t, 2, True, 16 * d, 16)], lambda d=d: ga.at[t, d],
                 lambda d=d: at_x(way[d]))

    def beyond(t):
        for d in range(2):
            joined(t, way[d])
            onto(t, d, 1)
        joined(t, 0)

    def onto(t, d, part):
        start = 16 * d if part == 0 else 16 * (1 - d)
        send(("gb", t, d, part), lambda: acc.at[block(t, way[d], True, start, 16)],
             lambda: gb.at[t, d, pl.ds(start, 16), :], lambda: at_x(way[d]))

    def second(t):
        for d in range(2):
            arrived(("ga", t, d), ga.at[t, d], at_x(way[d]))
            acc[block(t, way[d], True, 16 * d, 16)] += ga[t, d]
            onto(t, d, 0)

    def third(t):
        for d in range(2):
            for part in range(2):
                start = 16 * d if part == 0 else 16 * (1 - d)
                arrived(("gb", t, d, part), gb.at[t, d, pl.ds(start, 16), :], at_x(way[d]))
        g_out[:, t * WIDTH : (t + 1) * WIDTH] -= acc[block(t, 0, True)] + gb[t, 0] + gb[t, 1]

    def leave(items):
        for key, src, dst, to in items:
            make(key, src(), dst(), to()).wait_send()

    before_tail = list(sent)
    for t in range(TILES):
        to_partner(t)
    for t in range(TILES):
        first(t)
    for t in range(TILES):
        beyond(t)
    factor_all()
    for t in range(TILES):
        second(t)
    leave(before_tail)
    for d in range(1, 4):
        arrived(("t4", d), rows_of(t_all, lax.rem(z + 4 - d, 4), 8), at_z(d))
    t_hi, t_lo = halves(t_all[...])
    for t in range(TILES):
        cols = slice(t * WIDTH, (t + 1) * WIDTH)
        g_out[:, cols] = mm(t_hi, h_hi[:, cols]) + mm(t_hi, h_lo[:, cols]) + mm(t_lo, h_hi[:, cols])
    for d in range(1, 4):
        arrived(("a3", d), a3.at[lax.rem(z + 4 - d, 4)], at_z(d))
    stat_out[...] = (a3[0] + a3[1] + a3[2] + a3[3])[:2, :2]
    for t in range(TILES):
        third(t)
    leave(sent[len(before_tail) :])


def hand_over(w_in, g_in, stat_in, w_out, g_out, stat_out, out_sem):
    copies = [
        pltpu.make_async_copy(source, target, out_sem.at[n])
        for n, (source, target) in enumerate(((w_in, w_out), (g_in, g_out), (stat_in, stat_out)))
    ]
    for copy in copies:
        copy.start()
    for copy in copies:
        copy.wait()


def per_device(a_matrix, h_factor, w_factor, accept, shrink):
    vmem = pltpu.VMEM
    anywhere = pl.BlockSpec(memory_space=pl.ANY)
    inside = pl.BlockSpec(memory_space=vmem)
    results = pl.pallas_call(
        kernel,
        out_shape=(
            vmem((ROWS, RANK), F32),
            vmem((RANK // 8, COLS), F32),
            vmem((2, 2), F32),
        ),
        in_specs=[anywhere] * 5,
        out_specs=(inside, inside, inside),
        scratch_shapes=[
            vmem((2, GROUP, COLS), F32),
            vmem((ROWS, COLS), BF16),
            vmem((ROWS, COLS), BF16),
            vmem((RANK, COLS), F32),
            vmem((RANK, COLS), BF16),
            vmem((RANK, COLS), BF16),
            vmem((ROWS, RANK), F32),
            vmem((2, 2, 2, PIECE, RANK), F32),
            vmem((2, 2, 4, PIECE, RANK), F32),
            vmem((2, 2, 64, RANK), F32),
            vmem((2, 2, PIECE, RANK), F32),
            vmem((4, 32, RANK), F32),
            vmem((4, 32, RANK), F32),
            vmem((8, 32, RANK), F32),
            vmem((32, RANK), F32),
            vmem((4, 8, RANK), F32),
            vmem((4, 8, RANK), F32),
            vmem((32, RANK), F32),
            vmem((8, 32, RANK), F32),
            vmem((RANK, RANK), F32),
            vmem((2, ROWS), jnp.int32),
            vmem((2, ROWS), jnp.int32),
            vmem((2, RANK, PIECE), F32),
            vmem((2, RANK, PIECE), F32),
            vmem((RANK, RANK), F32),
            vmem((RANK, RANK), F32),
            vmem((TILES, RANK, WIDTH), F32),
            vmem((RANK, RANK), F32),
            vmem((TILES, 4, 32, WIDTH), F32),
            vmem((TILES, 2, 16, WIDTH), F32),
            vmem((TILES, 2, 32, WIDTH), F32),
            vmem((8, 8, 128), F32),
            vmem((4, 8, 128), F32),
            vmem((4, 8, 128), F32),
            pltpu.SemaphoreType.DMA((len(KEYS),)),
            pltpu.SemaphoreType.DMA((len(KEYS),)),
            pltpu.SemaphoreType.DMA((2,)),
            pltpu.SemaphoreType.DMA((5,)),
        ],
        compiler_params=pltpu.CompilerParams(
            collective_id=0, has_side_effects=True, vmem_limit_bytes=58 * 1024 * 1024
        ),
    )(a_matrix, h_factor, w_factor, accept.T, shrink.T)
    held = [pltpu.with_memory_space_constraint(result, vmem) for result in results]
    return pl.pallas_call(
        hand_over,
        out_shape=(
            jax.ShapeDtypeStruct((ROWS, RANK), F32),
            jax.ShapeDtypeStruct((RANK // 8, COLS), F32),
            jax.ShapeDtypeStruct((2, 2), F32),
        ),
        in_specs=[inside, inside, inside],
        out_specs=(anywhere, anywhere, anywhere),
        scratch_shapes=[pltpu.SemaphoreType.DMA((3,))],
        compiler_params=pltpu.CompilerParams(vmem_limit_bytes=8 * 1024 * 1024),
    )(*held)

def solution(mesh):
    in_specs = (P("row", "col"), P(None, "col"), P("row", None), P("row", None), P("row", None))
    out_specs = (P("row", None), P("row", "col"), P())
    return jax.shard_map(per_device, mesh=mesh, in_specs=in_specs, out_specs=out_specs, check_vma=False)
```
